768 devices in a mesh: slab: 96 (over z, x, core), depth: 8 (over y).
Axes of the slice: x: 4, y: 8, z: 12, core: 2. Of those that a mesh axis runs over, the one named last changes fastest.
Arguments:
- nutrient: float32 [768, 256, 512], P('slab', 'depth'), may hold values from 0.5 to 2
- species: bfloat16 [786432, 128], P(('slab', 'depth')), may hold values from -6 to 6
- agent_cell: int32 [786432], P(('slab', 'depth')), may hold values from 0 to 131071
- death_flag: int32 [786432], P(('slab', 'depth')), may hold values 0 or 1
- divide_flag: int32 [786432], P(('slab', 'depth')), may hold values 0 or 1
- slab_move: int32 [786432], P(('slab', 'depth')), may hold values from 0 to 2, as said below
- depth_route: int32 [786432, 1], P(('slab', 'depth')), may hold values from 0 to 7; in each aligned block of 1024 rows (0 to 1023, 1024 to 2047, ...) at most 256 rows name the same one
- net_weight: bfloat16 [128, 128], replicated, may hold values from -0.5 to 0.5
- sensing: float32 [128], replicated, may hold values from -1 to 1
- uptake_weight: bfloat16 [128], replicated, may hold values from -0.5 to 0.5
Outputs:
- nutrient_next: float32 [768, 256, 512], P('slab', 'depth')
- species_after_step: bfloat16 [1769472, 128], P(('slab', 'depth'))
The draws below stay inside these ranges and needn't reach their ends.
Inputs may be any that keep to these rules, and one draw needn't show every extreme that they name: `slab_move`: within each device's 1024 rows at most 128 carry 1 and at most 128 carry 2; some device has exactly 128 carrying 1 and some device exactly 128 carrying 2. `depth_route`: within each device's 1024 rows no depth index is named more than 256 times; one is named exactly 256 times in some device.
All inputs are finite; a program needn't handle non-finite values. No bound on the sum of `death_flag` or of `divide_flag` on one device may be relied on, other than what follows from the above.
Results may differ from the reference program's by a relative error of at most 0.0045.
Values may be sent and summed in bfloat16 or wider, within the bound.
A program may use at most 128 MiB of HBM per device.

```python
import math
import jax
import jax.numpy as jnp
import numpy as np
from jax import lax

SPECIES_COUNT = 128
CX = 8
CY = 32
CZ = 512
A_DEV = 1024
PRE = 2
COARSE = 4
MIG = 128
DEPTHS = 8
SLOT_CAPACITY = 256
NX = 768
NY = 256
NZ = 512
CELLS_DEV = 131072
AGENTS = 786432
N_SLAB = 96
N_DEPTH = 8


def draw_slab_move(key, part):
    block_count = AGENTS // A_DEV
    first_key, second_key, third_key = jax.random.split(key, 3)
    up_counts = jax.random.randint(first_key, (block_count,), MIG // 4, MIG + 1).at[0].set(MIG)
    down_counts = jax.random.randint(second_key, (block_count,), MIG // 4, MIG + 1).at[block_count - 1].set(MIG)
    block_keys = jax.random.split(third_key, block_count)

    def shuffle(block_key):
        return jax.random.permutation(block_key, A_DEV)
    ranks = jax.vmap(shuffle)(block_keys)
    move_code = jnp.where(ranks < up_counts[:, None], 1, jnp.where(ranks < (up_counts + down_counts)[:, None], 2, 0))
    return move_code.reshape(-1).astype(jnp.int32)


def place_ends(drawn, key, low, top_value):
    spot = [jax.random.randint(jax.random.fold_in(key, axis), (), 0, length) for axis, length in enumerate(drawn.shape)]
    main_axis = drawn.shape.index(max(drawn.shape))
    neighbour = spot[:main_axis] + [(spot[main_axis] + 1) % drawn.shape[main_axis]] + spot[main_axis + 1:]
    return drawn.at[tuple(spot)].set(low).at[tuple(neighbour)].set(top_value)


def steps_of(key, dims, shards, least, top_value):
    loudness = 1.0
    for position, blocks in shards:
        steps = jax.random.uniform(jax.random.fold_in(jax.random.fold_in(key, 6), position), (blocks,), jnp.float32, least / len(shards), top_value / len(shards))
        loudness = loudness * jnp.repeat(jnp.exp(steps), dims[position] // blocks).reshape((-1,) + (1,) * (len(dims) - 1 - position))
    return loudness


def routed_block(rng, own, number, rows, amount, top, limit, skew):
    order = jax.random.permutation(rng, amount)
    packed, usual = portions_of(amount, rows * top, limit, skew, True), portions_of(amount, rows * top, limit, skew, False)
    places = jnp.arange(amount)

    def named(sizes, offset_by):
        used = int((sizes > 0).sum())
        fixed = max(1, used // 4)
        shifted = fixed + (places - fixed + offset_by * (used - fixed)) % max(1, amount - fixed)
        return jnp.zeros((amount,), jnp.int32).at[order[jnp.where(places < fixed, places, shifted)]].set(jnp.asarray(sizes, jnp.int32))

    sizes = jnp.where(number % 4 == 0, named(packed, number // 4), named(usual, number - number // 4 - 1))
    mixed = jax.random.permutation(jax.random.fold_in(own, 3), amount)
    donor, taker = mixed[0:amount // 2 * 2:2], mixed[1:amount // 2 * 2:2]
    room = jnp.minimum(sizes[donor] - 1, limit - sizes[taker]) // 2
    room = jnp.where((donor == order[0]) | (taker == order[0]) | (sizes[taker] == 0), 0, jnp.maximum(room, 0))
    shifted = jax.random.randint(jax.random.fold_in(own, 4), (amount // 2,), 0, 1 << 20) % (room + 1)
    sizes = sizes.at[donor].add(-shifted).at[taker].add(shifted)
    labels = jnp.searchsorted(jnp.cumsum(sizes), jnp.arange(rows * top), side="right").astype(jnp.int32)
    table = labels.reshape(top, rows).T
    table = table[jax.random.permutation(jax.random.fold_in(own, 1), rows)]
    offset_by = jax.random.randint(jax.random.fold_in(own, 2), (rows, 1), 0, top)
    return jnp.take_along_axis(table, (jnp.arange(top)[None, :] + offset_by) % top, axis=1)


def portions_of(count, total, reach, skew, full):
    weights = [(1 << 20) // math.isqrt(standing ** skew) + 1 for standing in range(1, count + 1)]
    largest = reach if full else min(reach, max(-(-total // count), total * weights[0] // sum(weights)))
    least = 1 if total - largest >= count - 1 else 0
    given, surplus = [largest] + [least] * (count - 1), total - largest - least * (count - 1)
    while surplus > 0:
        movable = [i for i in range(1, count) if given[i] < largest] or [i for i in range(1, count) if given[i] < reach]
        mass, remaining = sum([weights[i] for i in movable]), surplus
        for i in movable:
            more = min(reach - given[i], max(1, remaining * weights[i] // mass), surplus)
            given[i] = given[i] + more
            surplus = surplus - more
    return np.array(given)


def scatter_about(key, dims, scale, most, pieces=(), held_as=jnp.bfloat16):
    drawn = scale * jax.random.normal(key, dims, jnp.float32)
    if pieces:
        drawn = drawn * steps_of(key, dims, pieces, -0.22, 0.18)
    return jnp.clip(drawn, -most, most).astype(held_as)


def setup_inputs(seed: int = 0) -> dict:
    key_of = jax.random.split(jax.random.key(seed), 11)
    nutrient = jnp.clip(0.5 + 1.5 * jax.random.uniform(key_of[0], (NX, NY, NZ), jnp.float32) ** steps_of(key_of[0], (NX, NY, NZ), ((0, 96), (1, 8)), -0.2, 0.2), 0.5, 2.0)
    species = scatter_about(key_of[1], (AGENTS, SPECIES_COUNT), 1.0, 6.0, ((0, 768),))
    agent_cell = place_ends(jax.random.randint(key_of[2], (AGENTS,), 0, CELLS_DEV), jax.random.fold_in(key_of[2], 1), 0, CELLS_DEV - 1).astype(jnp.int32)
    death_flag = place_ends((jax.random.randint(key_of[3], (AGENTS,), 0, 8) < 1).astype(jnp.int32), jax.random.fold_in(key_of[3], 1), 0, 1)
    divide_flag = place_ends((jax.random.randint(key_of[4], (AGENTS,), 0, 4) < 1).astype(jnp.int32), jax.random.fold_in(key_of[4], 1), 0, 1)
    slab_move = draw_slab_move(jax.random.fold_in(key_of[10], 71), 0)
    depth_route_keys = jax.random.split(jax.random.fold_in(key_of[6], 1), AGENTS // A_DEV)
    depth_route_turns = jax.random.permutation(jax.random.fold_in(key_of[6], 3), AGENTS // A_DEV)
    depth_route = jax.vmap(lambda own, number: routed_block(jax.random.fold_in(key_of[6], 2), own, number, A_DEV, DEPTHS, 1, SLOT_CAPACITY, 2))(depth_route_keys, depth_route_turns).reshape((AGENTS, 1))
    net_weight = scatter_about(key_of[7], (SPECIES_COUNT, SPECIES_COUNT), SPECIES_COUNT ** -0.5, 0.5)
    sensing = jnp.clip(jax.random.uniform(key_of[8], (SPECIES_COUNT,), jnp.float32, -1.0, 1.0), -1.0, 1.0)
    uptake_weight = scatter_about(key_of[9], (SPECIES_COUNT,), SPECIES_COUNT ** -0.5, 0.5)
    return dict(nutrient=nutrient, species=species, agent_cell=agent_cell, death_flag=death_flag, divide_flag=divide_flag, slab_move=slab_move, depth_route=depth_route, net_weight=net_weight, sensing=sensing, uptake_weight=uptake_weight)


SCREENING = 0.05
DAMPING = 2.0 / 3.0


def neighbour_sum(grid_field):
    along_first = jnp.roll(grid_field, 1, 0) + jnp.roll(grid_field, -1, 0)
    padded = jnp.pad(grid_field, ((0, 0), (1, 1), (1, 1)))
    along_second = padded[:, 2:, 1:-1] + padded[:, :-2, 1:-1]
    along_third = padded[:, 1:-1, 2:] + padded[:, 1:-1, :-2]
    return along_first + along_second + along_third


def relax_step(grid_field, target, centre):
    image_field = centre * grid_field - neighbour_sum(grid_field)
    return grid_field + DAMPING * (target - image_field) / centre


def reference(nutrient, species, agent_cell, death_flag, divide_flag, slab_move, depth_route, net_weight, sensing, uptake_weight):
    agent_rows = jnp.arange(AGENTS, dtype=jnp.int32)
    block_index = agent_rows // A_DEV
    slab_position_index = block_index // N_DEPTH
    depth_position_index = block_index % N_DEPTH
    cell_first = slab_position_index * CX + agent_cell // (CY * CZ)
    cell_second = depth_position_index * CY + (agent_cell // CZ) % CY
    cell_third = agent_cell % CZ
    sample = nutrient[cell_first, cell_second, cell_third]
    alive_mask = (1 - death_flag).astype(jnp.float32)
    uptake_score = jnp.dot(species, uptake_weight, preferred_element_type=jnp.float32)
    uptake = alive_mask * (1.0 + divide_flag.astype(jnp.float32)) * jax.nn.softplus(uptake_score) * sample / (0.5 + sample)
    source = jnp.zeros_like(nutrient).at[cell_first, cell_second, cell_third].add(uptake)
    target = SCREENING * nutrient - source
    centre = 6.0 + SCREENING
    grid_field = nutrient
    for sweep_step in range(PRE):
        grid_field = relax_step(grid_field, target, centre)
    residual = target - (centre * grid_field - neighbour_sum(grid_field))
    coarse_target = 4.0 * residual.reshape(NX // 2, 2, NY // 2, 2, NZ // 2, 2).mean(axis=(1, 3, 5))
    coarse = jnp.zeros_like(coarse_target)
    for sweep_step in range(COARSE):
        coarse = relax_step(coarse, coarse_target, 6.0 + 4.0 * SCREENING)
    grid_field = grid_field + jnp.repeat(jnp.repeat(jnp.repeat(coarse, 2, 0), 2, 1), 2, 2)
    for sweep_step in range(PRE):
        grid_field = relax_step(grid_field, target, centre)

    sensed = lax.optimization_barrier(sample.astype(jnp.bfloat16)).astype(jnp.float32)
    activation = jnp.dot(species, net_weight, preferred_element_type=jnp.float32) + sensed[:, None] * sensing[None, :]
    updated = (alive_mask[:, None] * (0.5 * species.astype(jnp.float32) + jnp.tanh(activation))).astype(jnp.bfloat16)

    target_device = depth_route[:, 0]
    dest_hits = (target_device[:, None] == jnp.arange(N_DEPTH, dtype=jnp.int32)[None, :]).astype(jnp.int32).reshape(-1, A_DEV, N_DEPTH)
    earlier = jnp.cumsum(dest_hits, axis=1) - dest_hits
    destination_slot = jnp.sum(earlier * dest_hits, axis=2).reshape(-1)
    remaining_agents = jnp.where((slab_move == 0)[:, None], updated, jnp.zeros_like(updated))
    balanced_slots = jnp.zeros((N_SLAB, N_DEPTH, N_DEPTH, SLOT_CAPACITY, SPECIES_COUNT), jnp.bfloat16).at[slab_position_index, target_device, depth_position_index, destination_slot].set(remaining_agents)

    def pack_movers(move_code, shift_by):
        chosen = (slab_move == move_code).astype(jnp.int32).reshape(-1, A_DEV)
        rank_order = (jnp.cumsum(chosen, axis=1) - chosen).reshape(-1)
        target_slot = jnp.where(chosen.reshape(-1) == 1, rank_order, MIG)
        buffer = jnp.zeros((N_SLAB, N_DEPTH, MIG, SPECIES_COUNT), jnp.bfloat16)
        return buffer.at[(slab_position_index + shift_by) % N_SLAB, depth_position_index, target_slot].set(updated, mode="drop")

    incoming_below = pack_movers(1, 1)
    incoming_above = pack_movers(2, -1)
    species_after_step = jnp.concatenate([balanced_slots.reshape(N_SLAB, N_DEPTH, N_DEPTH * SLOT_CAPACITY, SPECIES_COUNT), incoming_below, incoming_above], axis=2)
    return grid_field, species_after_step.reshape(-1, SPECIES_COUNT)
```

```python
import functools

import jax
import jax.numpy as jnp
from jax import lax
from jax.experimental import pallas as pl
from jax.experimental.pallas import tpu as pltpu
from jax.sharding import PartitionSpec as P

SCREENING = 0.05
DAMPING = 2.0 / 3.0
CENTRE = 6.0 + SCREENING
COARSE_CENTRE = 6.0 + 4.0 * SCREENING
F32 = jnp.float32
BF16 = jnp.bfloat16
I32 = jnp.int32
MESH = pl.DeviceIdType.MESH
HIGHEST = lax.Precision.HIGHEST

ROWS = 1024
CAP = 256
MIG = 128
WIDTH = 128
SIDES = ((1, 0), (-1, 0), (0, 1), (0, -1), (1, 1), (1, -1), (-1, 1), (-1, -1))


def iota(shape, axis, dtype=I32):
    values = lax.broadcasted_iota(I32, shape, axis)
    return values if dtype == I32 else values.astype(dtype)


def neighbour_sum(centre, below, above, first_lane, last_lane):
    rows, lanes = centre.shape
    left = jnp.where(first_lane, 0.0, pltpu.roll(centre, 1, 1))
    right = jnp.where(last_lane, 0.0, pltpu.roll(centre, lanes - 1, 1))
    low = pltpu.roll(centre, 1, 0)
    high = pltpu.roll(centre, rows - 1, 0)
    return (below + above) + (low + high) + (left + right)


def kernel(
    n_slab, n_depth,
    nut, spec, cell, death, divide, move, route, netw, sensing, uw,
    grid_out, spec_out,
    nb, nb_low, nb_high, src, src_low, src_high, cb, cb_low, cb_high,
    xr_low, xr_high, yr_low, yr_high,
    xs_low, xs_high, ys_low, ys_high,
    xc_low, xc_high, yc_low, yc_high,
    lane_hot, upd, packed, movers, sbuf, tbuf, ubuf, vbuf, rbuf, cbuf, dbuf, ebuf,
    halo_send, halo_recv, a2a_send, a2a_recv, mig_send, mig_recv,
):
    s = lax.axis_index("slab")
    d = lax.axis_index("depth")

    def at(step_s, step_d):
        return (lax.rem(s + step_s + n_slab, n_slab), lax.rem(d + step_d + n_depth, n_depth))

    barrier = pltpu.get_barrier_semaphore()
    partners = [at(a, b) for a, b in SIDES if a != 0] + [at(0, k) for k in range(1, n_depth)]
    for partner in partners:
        pl.semaphore_signal(barrier, inc=1, device_id=partner, device_id_type=MESH)

    def exchange(number, sources, targets):
        copies = []
        for i, (a, b) in enumerate(SIDES):
            copy = pltpu.make_async_remote_copy(
                src_ref=sources[i],
                dst_ref=targets[i],
                send_sem=halo_send.at[number, i],
                recv_sem=halo_recv.at[number, i],
                device_id=at(a, b),
                device_id_type=MESH,
            )
            copy.start()
            copies.append(copy)
        return copies

    for x in range(8):
        plane = nut[x].astype(BF16)
        nb[x] = plane
        nb_low[x] = plane[0:4]
        nb_high[x] = plane[28:32]

    cell_row = cell[...]
    z_row = lax.rem(cell_row, 512)
    xy_row = lax.div(cell_row, 512)

    def fill_lane(i, carry):
        start = pl.multiple_of(i * 64, 64)
        hit = (iota((64, ROWS), 0) + start) == z_row
        lane_hot[pl.ds(start, 64), :] = jnp.where(hit, 1.0, 0.0).astype(BF16)
        return carry

    lax.fori_loop(0, 8, fill_lane, 0)
    sampled = jnp.dot(nb[...].reshape(256, 512), lane_hot[...], preferred_element_type=F32)
    row_hit = iota((256, ROWS), 0) == xy_row
    sample = jnp.sum(jnp.where(row_hit, sampled, 0.0), axis=0, keepdims=True)

    alive = 1.0 - death[...].astype(F32)
    score = lax.dot_general(
        jnp.broadcast_to(uw[...], (16, WIDTH)), spec[...], (((1,), (1,)), ((), ())),
        preferred_element_type=F32,
    )[0:1]
    softplus = jnp.maximum(score, 0.0) + jnp.log1p(jnp.exp(-jnp.abs(score)))
    uptake = alive * (1.0 + divide[...].astype(F32)) * softplus * sample / (0.5 + sample)

    pl.semaphore_wait(barrier, len(partners))
    first = exchange(
        0,
        [nb.at[pl.ds(4, 4)], nb.at[pl.ds(0, 4)], nb_high, nb_low,
         nb_high.at[pl.ds(4, 4)], nb_low.at[pl.ds(4, 4)],
         nb_high.at[pl.ds(0, 4)], nb_low.at[pl.ds(0, 4)]],
        [xr_low, xr_high, yr_low.at[pl.ds(4, 8)], yr_high.at[pl.ds(4, 8)],
         yr_low.at[pl.ds(0, 4)], yr_high.at[pl.ds(0, 4)],
         yr_low.at[pl.ds(12, 4)], yr_high.at[pl.ds(12, 4)]],
    )

    piece = uptake.astype(BF16).astype(F32)
    rest = uptake - piece
    row_hit = iota((256, ROWS), 0) == xy_row
    pieces = jnp.concatenate(
        [jnp.where(row_hit, piece, 0.0).astype(BF16), jnp.where(row_hit, rest, 0.0).astype(BF16)],
        axis=0,
    )
    sources = lax.dot_general(
        pieces, lane_hot[...], (((1,), (1,)), ((), ())), preferred_element_type=F32
    )
    source = (sources[0:256] + sources[256:512]).reshape(8, 32, 512)
    for x in range(8):
        plane = source[x]
        rounded = plane.astype(BF16)
        src[x] = rounded
        src_low[x] = rounded[0:4]
        src_high[x] = rounded[28:32]
        ubuf[4 + x, 0:32, :] = nut[x]
        tbuf[4 + x, 0:32, :] = SCREENING * nut[x] - plane
    second = exchange(
        1,
        [src.at[pl.ds(5, 3)], src.at[pl.ds(0, 3)], src_high, src_low,
         src_high.at[pl.ds(5, 3)], src_low.at[pl.ds(5, 3)],
         src_high.at[pl.ds(0, 3)], src_low.at[pl.ds(0, 3)]],
        [xs_low.at[pl.ds(1, 3)], xs_high.at[pl.ds(0, 3)],
         ys_low.at[pl.ds(4, 8)], ys_high.at[pl.ds(4, 8)],
         ys_low.at[pl.ds(1, 3)], ys_high.at[pl.ds(1, 3)],
         ys_low.at[pl.ds(12, 3)], ys_high.at[pl.ds(12, 3)]],
    )

    sensed = sample.astype(BF16).astype(F32)
    activation = jnp.dot(spec[...], netw[...], preferred_element_type=F32)
    sensed_column = jnp.transpose(jnp.broadcast_to(sensed, (WIDTH, ROWS)))
    activation = activation + sensed_column * sensing[...]
    upd[...] = (0.5 * spec[...].astype(F32) + jnp.tanh(activation)).astype(BF16)

    lanes = iota((16, ROWS), 0)
    move_row = move[...]
    route_row = route[...]
    counted = (lanes == route_row) | (lanes == 7 + move_row) & (move_row > 0)
    counted = jnp.where(counted, 1.0, 0.0)
    chosen = jnp.where(move_row == 0, route_row, 7 + move_row)
    stacked = jnp.concatenate([counted[:, a * 128:(a + 1) * 128] for a in range(8)], axis=0)
    before = jnp.where(iota((128, 128), 0) < iota((128, 128), 1), 1.0, 0.0)
    inside = jnp.dot(stacked.astype(BF16), before.astype(BF16), preferred_element_type=F32)
    total = jnp.dot(stacked.astype(BF16), jnp.ones((128, 128), BF16), preferred_element_type=F32)
    offset = jnp.zeros((16, 128), F32)
    ranks = []
    for a in range(8):
        ranks.append(inside[a * 16:(a + 1) * 16] + offset)
        offset = offset + total[a * 16:(a + 1) * 16]
    rank = jnp.concatenate(ranks, axis=1)
    rank = jnp.sum(jnp.where(lanes == chosen, rank, 0.0), axis=0, keepdims=True)
    rank = jnp.where(alive > 0.0, rank, -1.0)
    chosen = chosen.astype(F32)

    def pack(destination, slots):
        key = jnp.where(chosen == destination, rank, -1.0)
        hot = jnp.where(iota((slots, ROWS), 0, F32) == key, 1.0, 0.0).astype(BF16)
        return jnp.dot(hot, upd[...], preferred_element_type=F32).astype(BF16)

    def pack_step(k, carry):
        packed[k] = pack(lax.rem(d + k, n_depth).astype(F32), CAP)
        return carry

    lax.fori_loop(1, n_depth, pack_step, 0)
    movers[0] = pack(8.0, MIG)
    movers[1] = pack(9.0, MIG)
    own = pl.multiple_of(d * CAP, CAP)
    spec_out[pl.ds(own, CAP), :] = pack(d.astype(F32), CAP)

    def send_block(k):
        copy = pltpu.make_async_remote_copy(
            src_ref=packed.at[k],
            dst_ref=spec_out.at[pl.ds(own, CAP), :],
            send_sem=a2a_send.at[k],
            recv_sem=a2a_recv.at[k],
            device_id=at(0, k),
            device_id_type=MESH,
        )
        copy.start()
        return copy

    blocks = [send_block(k) for k in (4, 3, 5)]

    lane = iota((1, 512), 1)
    first_lane = lane == 0
    last_lane = lane == 511
    row8 = iota((8, 1), 0)
    inside_domain = ((row8 < 4) & (d < n_depth - 1)) | ((row8 >= 4) & (d > 0))
    for copy in first + second:
        copy.wait_recv()

    def halo_rows(high, low):
        joined = jnp.concatenate([high.astype(F32), low.astype(F32)], axis=0)
        return jnp.where(inside_domain, joined, 0.0)

    def outer(x, low, high, s_low, s_high, i):
        value = (low if low is not None else high)[i].astype(F32)
        ubuf[x, 0:32, :] = value
        tbuf[x, 0:32, :] = SCREENING * value - (s_low if s_low is not None else s_high)[i].astype(F32)

    for i in range(1, 4):
        outer(i, xr_low, None, xs_low, None, i)
    for i in range(0, 3):
        outer(12 + i, None, xr_high, None, xs_high, i)
    ubuf[0, 0:32, :] = xr_low[0].astype(F32)
    ubuf[15, 0:32, :] = xr_high[3].astype(F32)

    def fill_rows(x, carry):
        value = halo_rows(yr_high[x], yr_low[x])
        ubuf[x, 32:40, :] = value
        tbuf[x, 32:40, :] = SCREENING * value - halo_rows(ys_high[x], ys_low[x])
        return carry

    lax.fori_loop(0, 16, fill_rows, 0)

    def masked(value):
        rows = value.shape[0] - 8
        return jnp.concatenate([value[0:rows], jnp.where(inside_domain, value[rows:], 0.0)], axis=0)

    def sweep(source_ref, x):
        value = source_ref[x]
        around = neighbour_sum(value, source_ref[x - 1], source_ref[x + 1], first_lane, last_lane)
        return value * (1.0 - DAMPING) + (DAMPING / CENTRE) * (tbuf[x] + around)

    def sweep_first(x, carry):
        vbuf[x] = masked(sweep(ubuf, x))
        return carry

    def sweep_second(x, carry):
        ubuf[x] = masked(sweep(vbuf, x))
        return carry

    lax.fori_loop(1, 15, sweep_first, 0)
    lax.fori_loop(2, 14, sweep_second, 0)

    def residual(x, carry):
        value = ubuf[x]
        around = neighbour_sum(value, ubuf[x - 1], ubuf[x + 1], first_lane, last_lane)
        rbuf[x - 4] = tbuf[x, 0:32, :] - (CENTRE * value - around)[0:32]
        return carry

    lax.fori_loop(4, 12, residual, 0)

    planes = jnp.concatenate([rbuf[2 * p] + rbuf[2 * p + 1] for p in range(4)], axis=0)
    lane_pairs = jnp.where(lax.div(iota((512, 256), 0), 2) == iota((512, 256), 1), 1.0, 0.0)
    row_pairs = jnp.where(iota((64, 128), 0) == lax.div(iota((64, 128), 1), 2), 1.0, 0.0)
    halved = jnp.dot(planes, lane_pairs, preferred_element_type=F32, precision=HIGHEST)
    coarse_target = 0.5 * jnp.dot(row_pairs, halved, preferred_element_type=F32, precision=HIGHEST)
    for p in range(4):
        plane = coarse_target[p * 16:(p + 1) * 16]
        rounded = plane.astype(BF16)
        cb[p] = rounded
        cb_low[p] = rounded[0:4]
        cb_high[p] = rounded[12:16]
        cbuf[4 + p, 0:16, :] = plane
    third = exchange(
        2,
        [cb, cb, cb_high, cb_low, cb_high, cb_low, cb_high, cb_low],
        [xc_low, xc_high, yc_low.at[pl.ds(4, 4)], yc_high.at[pl.ds(4, 4)],
         yc_low.at[pl.ds(0, 4)], yc_high.at[pl.ds(0, 4)],
         yc_low.at[pl.ds(8, 4)], yc_high.at[pl.ds(8, 4)]],
    )
    blocks += [send_block(k) for k in (2, 6, 1, 7)]
    moved = []
    for i, step in enumerate((1, -1)):
        copy = pltpu.make_async_remote_copy(
            src_ref=movers.at[i],
            dst_ref=spec_out.at[pl.ds(n_depth * CAP + i * MIG, MIG), :],
            send_sem=mig_send.at[i],
            recv_sem=mig_recv.at[i],
            device_id=at(step, 0),
            device_id_type=MESH,
        )
        copy.start()
        moved.append(copy)
    for copy in third:
        copy.wait_recv()

    for p in range(4):
        cbuf[p, 0:16, :] = xc_low[p].astype(F32)
        cbuf[8 + p, 0:16, :] = xc_high[p].astype(F32)
    for p in range(12):
        cbuf[p, 16:24, :] = halo_rows(yc_high[p], yc_low[p])
    c_lane = iota((1, 256), 1)
    c_first = c_lane == 0
    c_last = c_lane == 255
    for p in range(12):
        dbuf[p] = (DAMPING / COARSE_CENTRE) * cbuf[p]

    def coarse_sweep(source_ref, target_ref, begin, end):
        def step(p, carry):
            value = source_ref[p]
            around = neighbour_sum(value, source_ref[p - 1], source_ref[p + 1], c_first, c_last)
            target_ref[p] = masked(
                value * (1.0 - DAMPING) + (DAMPING / COARSE_CENTRE) * (cbuf[p] + around)
            )
            return carry

        lax.fori_loop(begin, end, step, 0)

    coarse_sweep(dbuf, ebuf, 1, 11)
    coarse_sweep(ebuf, dbuf, 2, 10)
    coarse_sweep(dbuf, ebuf, 3, 9)

    fine_row = iota((40, 24), 0)
    from_row = jnp.where(fine_row < 36, lax.div(fine_row, 2), 22 + lax.div(fine_row - 36, 2))
    repeat_rows = jnp.where(from_row == iota((40, 24), 1), 1.0, 0.0)
    repeat_lanes = jnp.where(iota((256, 512), 0) == lax.div(iota((256, 512), 1), 2), 1.0, 0.0)
    spread = jnp.concatenate(
        [
            jnp.dot(repeat_rows, ebuf[3 + p], preferred_element_type=F32, precision=HIGHEST)
            for p in range(6)
        ],
        axis=0,
    )
    sbuf[...] = jnp.dot(
        spread, repeat_lanes, preferred_element_type=F32, precision=HIGHEST
    ).reshape(6, 40, 512)

    def correct(p, carry):
        addition = sbuf[p]
        ubuf[2 + 2 * p] = ubuf[2 + 2 * p] + addition
        ubuf[3 + 2 * p] = ubuf[3 + 2 * p] + addition
        return carry

    lax.fori_loop(0, 6, correct, 0)
    lax.fori_loop(3, 13, sweep_first, 0)

    def sweep_last(x, carry):
        value = vbuf[x]
        around = neighbour_sum(value, vbuf[x - 1], vbuf[x + 1], first_lane, last_lane)
        result = value * (1.0 - DAMPING) + (DAMPING / CENTRE) * (tbuf[x] + around)
        grid_out[x - 4] = result[0:32]
        return carry

    lax.fori_loop(4, 12, sweep_last, 0)

    for copy in blocks + moved:
        copy.wait_recv()
    for copy in first + second + third + blocks + moved:
        copy.wait_send()


def local(n_slab, n_depth, nutrient, species, agent_cell, death_flag, divide_flag, slab_move,
          depth_route, net_weight, sensing, uptake_weight):
    row = (1, ROWS)
    vmem = pl.BlockSpec(memory_space=pltpu.VMEM)
    scratch = [
        ((8, 32, 512), BF16), ((8, 4, 512), BF16), ((8, 4, 512), BF16),
        ((8, 32, 512), BF16), ((8, 4, 512), BF16), ((8, 4, 512), BF16),
        ((4, 16, 256), BF16), ((4, 4, 256), BF16), ((4, 4, 256), BF16),
        ((4, 32, 512), BF16), ((4, 32, 512), BF16), ((16, 4, 512), BF16), ((16, 4, 512), BF16),
        ((4, 32, 512), BF16), ((4, 32, 512), BF16), ((16, 4, 512), BF16), ((16, 4, 512), BF16),
        ((4, 16, 256), BF16), ((4, 16, 256), BF16), ((12, 4, 256), BF16), ((12, 4, 256), BF16),
        ((512, ROWS), BF16), ((ROWS, WIDTH), BF16), ((n_depth, CAP, WIDTH), BF16),
        ((2, MIG, WIDTH), BF16), ((6, 40, 512), F32),
        ((16, 40, 512), F32), ((16, 40, 512), F32), ((16, 40, 512), F32),
        ((8, 32, 512), F32), ((12, 24, 256), F32), ((12, 24, 256), F32), ((12, 24, 256), F32),
    ]
    return pl.pallas_call(
        functools.partial(kernel, n_slab, n_depth),
        out_shape=(
            jax.ShapeDtypeStruct((8, 32, 512), F32),
            jax.ShapeDtypeStruct((n_depth * CAP + 2 * MIG, WIDTH), BF16),
        ),
        in_specs=[vmem] * 10,
        out_specs=(vmem, vmem),
        scratch_shapes=[pltpu.VMEM(shape, dtype) for shape, dtype in scratch] + [
            pltpu.SemaphoreType.DMA((3, 8)), pltpu.SemaphoreType.DMA((3, 8)),
            pltpu.SemaphoreType.DMA((n_depth,)), pltpu.SemaphoreType.DMA((n_depth,)),
            pltpu.SemaphoreType.DMA((2,)), pltpu.SemaphoreType.DMA((2,)),
        ],
        compiler_params=pltpu.CompilerParams(
            collective_id=0, has_side_effects=True, vmem_limit_bytes=48 * 1024 * 1024
        ),
        name="step",
    )(
        nutrient, species, agent_cell.reshape(row), death_flag.reshape(row),
        divide_flag.reshape(row), slab_move.reshape(row), depth_route.reshape(row),
        net_weight, sensing.reshape(1, WIDTH), uptake_weight.reshape(1, WIDTH),
    )


def solution(mesh):
    in_specs = (
        P("slab", "depth", None),
        P(("slab", "depth"), None),
        P(("slab", "depth")),
        P(("slab", "depth")),
        P(("slab", "depth")),
        P(("slab", "depth")),
        P(("slab", "depth"), None),
        P(),
        P(),
        P(),
    )
    out_specs = (P("slab", "depth", None), P(("slab", "depth"), None))
    body = functools.partial(local, mesh.shape["slab"], mesh.shape["depth"])
    return jax.shard_map(body, mesh=mesh, in_specs=in_specs, out_specs=out_specs, check_vma=False)
```

```python
import functools

import jax
import jax.numpy as jnp
from jax import lax
from jax.experimental import pallas as pl
from jax.experimental.pallas import tpu as pltpu
from jax.sharding import PartitionSpec as P

SCREENING = 0.05
DAMPING = 2.0 / 3.0
CENTRE = 6.0 + SCREENING
COARSE_CENTRE = 6.0 + 4.0 * SCREENING
F32 = jnp.float32
BF16 = jnp.bfloat16
I32 = jnp.int32
MESH = pl.DeviceIdType.MESH

ROWS = 1024
CAP = 256
MIG = 128
WIDTH = 128
SIDES = ((1, 0), (-1, 0), (0, 1), (0, -1), (1, 1), (1, -1), (-1, 1), (-1, -1))


def iota(shape, axis, dtype=I32):
    values = lax.broadcasted_iota(I32, shape, axis)
    return values if dtype == I32 else values.astype(dtype)


def tile_sweep(ref, x, tiles, first_row, rows, first_lane, last_lane):
    centre = [ref[x, z, pl.ds(first_row, rows), :] for z in range(tiles)]
    ahead = [pltpu.roll(value, 1, 1) for value in centre]
    back = [pltpu.roll(value, 127, 1) for value in centre]
    out = []
    for z in range(tiles):
        left = jnp.where(first_lane, ahead[z - 1] if z > 0 else 0.0, ahead[z])
        right = jnp.where(last_lane, back[z + 1] if z < tiles - 1 else 0.0, back[z])
        total = left + right
        total = total + ref[x, z, pl.ds(first_row - 1, rows), :]
        total = total + ref[x, z, pl.ds(first_row + 1, rows), :]
        total = total + ref[x - 1, z, pl.ds(first_row, rows), :]
        total = total + ref[x + 1, z, pl.ds(first_row, rows), :]
        out.append((centre[z], total))
    return out


def kernel(
    n_slab, n_depth,
    nut_in, spec_in, cell_in, death_in, divide_in, move_in, route_in, netw_in, sensing_in, uw_in,
    grid_out, spec_out,
    nut, spec, cell, death, divide, move, route, netw, sensing, uw,
    nb, nb_low, nb_high, src, src_low, src_high, cb, cb_low, cb_high,
    xr_low, xr_high, yr_low, yr_high,
    xs_low, xs_high, ys_low, ys_high,
    xc_low, xc_high, yc_low, yc_high,
    lane_hot, upd, packed, movers, sbuf, tbuf, ubuf, vbuf, wbuf, rbuf, cbuf, dbuf, ebuf,
    halo_send, halo_recv, a2a_send, a2a_recv, mig_send, mig_recv, in_sem,
):
    s = lax.axis_index("slab")
    d = lax.axis_index("depth")

    def at(step_s, step_d):
        return (lax.rem(s + step_s + n_slab, n_slab), lax.rem(d + step_d + n_depth, n_depth))

    barrier = pltpu.get_barrier_semaphore()
    partners = [at(a, b) for a, b in SIDES if a != 0] + [at(0, k) for k in range(1, n_depth)]
    for partner in partners:
        pl.semaphore_signal(barrier, inc=1, device_id=partner, device_id_type=MESH)

    loads = []
    for i, (source_ref, target_ref) in enumerate((
        (cell_in, cell), (nut_in, nut), (spec_in, spec), (uw_in, uw), (death_in, death),
        (divide_in, divide), (move_in, move), (route_in, route), (netw_in, netw),
        (sensing_in, sensing),
    )):
        load = pltpu.make_async_copy(source_ref, target_ref, in_sem.at[i])
        load.start()
        loads.append(load)

    def exchange(number, sources, targets):
        copies = []
        for i, (a, b) in enumerate(SIDES):
            copy = pltpu.make_async_remote_copy(
                src_ref=sources[i],
                dst_ref=targets[i],
                send_sem=halo_send.at[number, i],
                recv_sem=halo_recv.at[number, i],
                device_id=at(a, b),
                device_id_type=MESH,
            )
            copy.start()
            copies.append(copy)
        return copies

    loads[0].wait()
    cell_row = cell[...]
    z_row = lax.rem(cell_row, 512)
    xy_row = lax.div(cell_row, 512)

    def fill_lane(i, carry):
        start = pl.multiple_of(i * 64, 64)
        hit = iota((64, ROWS), 0) == z_row - start
        lane_hot[pl.ds(start, 64), :] = jnp.where(hit, 1.0, 0.0).astype(BF16)
        return carry

    lax.fori_loop(0, 8, fill_lane, 0)

    loads[1].wait()
    for x in range(8):
        plane = nut[x].astype(BF16)
        nb[x] = plane
        nb_low[x] = plane[0:4]
        nb_high[x] = plane[28:32]
    pl.semaphore_wait(barrier, len(partners))
    first = exchange(
        0,
        [nb.at[pl.ds(4, 4)], nb.at[pl.ds(0, 4)], nb_high, nb_low,
         nb_high.at[pl.ds(4, 4)], nb_low.at[pl.ds(4, 4)],
         nb_high.at[pl.ds(0, 4)], nb_low.at[pl.ds(0, 4)]],
        [xr_low, xr_high, yr_low.at[pl.ds(4, 8)], yr_high.at[pl.ds(4, 8)],
         yr_low.at[pl.ds(0, 4)], yr_high.at[pl.ds(0, 4)],
         yr_low.at[pl.ds(12, 4)], yr_high.at[pl.ds(12, 4)]],
    )

    sampled = jnp.dot(nb[...].reshape(256, 512), lane_hot[...], preferred_element_type=F32)
    row_hit = iota((256, ROWS), 0) == xy_row
    sample = jnp.sum(jnp.where(row_hit, sampled, 0.0), axis=0, keepdims=True)
    for load in loads[2:]:
        load.wait()
    alive = 1.0 - death[...].astype(F32)
    score = lax.dot_general(
        jnp.broadcast_to(uw[...], (16, WIDTH)), spec[...], (((1,), (1,)), ((), ())),
        preferred_element_type=F32,
    )[0:1]
    softplus = jnp.maximum(score, 0.0) + jnp.log1p(jnp.exp(-jnp.abs(score)))
    uptake = alive * (1.0 + divide[...].astype(F32)) * softplus * sample / (0.5 + sample)

    row_hit = iota((256, ROWS), 0) == xy_row
    source = lax.dot_general(
        jnp.where(row_hit, uptake, 0.0).astype(BF16), lane_hot[...], (((1,), (1,)), ((), ())),
        preferred_element_type=F32,
    ).reshape(8, 32, 512)
    for x in range(8):
        plane = source[x]
        rounded = plane.astype(BF16)
        src[x] = rounded
        src_low[x] = rounded[0:4]
        src_high[x] = rounded[28:32]
        target = SCREENING * nut[x] - plane
        for z in range(4):
            tbuf[4 + x, z, 12:44, :] = target[:, z * 128:(z + 1) * 128]
    second = exchange(
        1,
        [src.at[pl.ds(5, 3)], src.at[pl.ds(0, 3)], src_high, src_low,
         src_high.at[pl.ds(5, 3)], src_low.at[pl.ds(5, 3)],
         src_high.at[pl.ds(0, 3)], src_low.at[pl.ds(0, 3)]],
        [xs_low.at[pl.ds(1, 3)], xs_high.at[pl.ds(0, 3)],
         ys_low.at[pl.ds(4, 8)], ys_high.at[pl.ds(4, 8)],
         ys_low.at[pl.ds(1, 3)], ys_high.at[pl.ds(1, 3)],
         ys_low.at[pl.ds(12, 3)], ys_high.at[pl.ds(12, 3)]],
    )
    for x in range(8):
        for z in range(4):
            ubuf[4 + x, z, 12:44, :] = nut[x, :, z * 128:(z + 1) * 128]

    sensed = sample.astype(BF16).astype(F32)
    activation = jnp.dot(spec[...], netw[...], preferred_element_type=F32)
    sensed_column = jnp.transpose(jnp.broadcast_to(sensed, (WIDTH, ROWS)))
    activation = activation + sensed_column * sensing[...]
    upd[...] = (0.5 * spec[...].astype(F32) + jnp.tanh(activation)).astype(BF16)

    lanes = iota((16, ROWS), 0)
    move_row = move[...]
    route_row = route[...]
    counted = (lanes == route_row) | (lanes == 7 + move_row) & (move_row > 0)
    counted = jnp.where(counted, 1.0, 0.0)
    chosen = jnp.where(move_row == 0, route_row, 7 + move_row)
    stacked = jnp.concatenate([counted[:, a * 128:(a + 1) * 128] for a in range(8)], axis=0)
    before = jnp.where(iota((128, 128), 0) < iota((128, 128), 1), 1.0, 0.0)
    inside = jnp.dot(stacked.astype(BF16), before.astype(BF16), preferred_element_type=F32)
    total = jnp.dot(stacked.astype(BF16), jnp.ones((128, 128), BF16), preferred_element_type=F32)
    offset = jnp.zeros((16, 128), F32)
    ranks = []
    for a in range(8):
        ranks.append(inside[a * 16:(a + 1) * 16] + offset)
        offset = offset + total[a * 16:(a + 1) * 16]
    rank = jnp.concatenate(ranks, axis=1)
    rank = jnp.sum(jnp.where(lanes == chosen, rank, 0.0), axis=0, keepdims=True)
    rank = jnp.where(alive > 0.0, rank, -1.0)
    chosen = chosen.astype(F32)

    def pack(destination, slots):
        key = jnp.where(chosen == destination, rank, -1.0)
        hot = jnp.where(iota((slots, ROWS), 0, F32) == key, 1.0, 0.0).astype(BF16)
        return jnp.dot(hot, upd[...], preferred_element_type=F32).astype(BF16)

    def pack_step(k, carry):
        packed[k] = pack(lax.rem(d + k, n_depth).astype(F32), CAP)
        return carry

    lax.fori_loop(1, n_depth, pack_step, 0)
    movers[0] = pack(8.0, MIG)
    movers[1] = pack(9.0, MIG)
    own = pl.multiple_of(d * CAP, CAP)
    spec_out[pl.ds(own, CAP), :] = pack(d.astype(F32), CAP)

    def send_block(k):
        copy = pltpu.make_async_remote_copy(
            src_ref=packed.at[k],
            dst_ref=spec_out.at[pl.ds(own, CAP), :],
            send_sem=a2a_send.at[k],
            recv_sem=a2a_recv.at[k],
            device_id=at(0, k),
            device_id_type=MESH,
        )
        copy.start()
        return copy

    blocks = [send_block(k) for k in (4, 3, 5)]

    lane = iota((1, 128), 1)
    first_lane = lane == 0
    last_lane = lane == 127
    row8 = iota((8, 1), 0)
    keep_low = (row8 >= 4) | (d > 0)
    keep_high = (row8 < 4) | (d < n_depth - 1)
    has_low = jnp.full((4, 1), d, I32) > 0
    has_high = jnp.full((4, 1), d, I32) < n_depth - 1

    def fill_rows(x, with_source):
        low = jnp.where(has_low, yr_low[x].astype(F32), 0.0)
        high = jnp.where(has_high, yr_high[x].astype(F32), 0.0)
        for z in range(4):
            at_z = slice(z * 128, (z + 1) * 128)
            ubuf[x, z, 8:12, :] = low[:, at_z]
            ubuf[x, z, 44:48, :] = high[:, at_z]
        if with_source:
            low = SCREENING * low - ys_low[x].astype(F32)
            high = SCREENING * high - ys_high[x].astype(F32)
            for z in range(4):
                at_z = slice(z * 128, (z + 1) * 128)
                tbuf[x, z, 8:12, :] = low[:, at_z]
                tbuf[x, z, 44:48, :] = high[:, at_z]

    def masked(value, rows):
        return jnp.concatenate(
            [jnp.where(keep_low, value[0:8], 0.0), value[8:rows - 8],
             jnp.where(keep_high, value[rows - 8:], 0.0)], axis=0,
        )

    def sweep(source_ref, target_ref, x):
        for z, (value, around) in enumerate(
            tile_sweep(source_ref, x, 4, 8, 40, first_lane, last_lane)
        ):
            result = value * (1.0 - DAMPING) + (DAMPING / CENTRE) * (tbuf[x, z, 8:48, :] + around)
            target_ref[x, z, 8:48, :] = masked(result, 40)

    def residual(x):
        for z, (value, around) in enumerate(
            tile_sweep(wbuf, x, 4, 12, 32, first_lane, last_lane)
        ):
            rbuf[x - 4, z] = tbuf[x, z, 12:44, :] + around - CENTRE * value

    def loop(begin, end, step):
        lax.fori_loop(begin, end, lambda x, carry: (step(x), carry)[1], 0)

    for copy in (first[2], first[3], second[2], second[3]):
        copy.wait_recv()
    loop(4, 12, lambda x: fill_rows(x, True))
    loop(5, 11, lambda x: sweep(ubuf, vbuf, x))
    loop(6, 10, lambda x: sweep(vbuf, wbuf, x))
    loop(7, 9, residual)

    for i in (0, 1, 4, 5, 6, 7):
        first[i].wait_recv()
        second[i].wait_recv()

    def fill_plane(x, value, taken):
        value = value.astype(F32)
        for z in range(4):
            ubuf[x, z, 12:44, :] = value[:, z * 128:(z + 1) * 128]
        if taken is not None:
            value = SCREENING * value - taken.astype(F32)
            for z in range(4):
                tbuf[x, z, 12:44, :] = value[:, z * 128:(z + 1) * 128]
        fill_rows(x, taken is not None)

    fill_plane(0, xr_low[0], None)
    fill_plane(15, xr_high[3], None)

    def fill_outer(i):
        fill_plane(i, xr_low[i], xs_low[i])
        fill_plane(11 + i, xr_high[i - 1], xs_high[i - 1])

    loop(1, 4, fill_outer)

    def both(step, offset):
        def run(x):
            step(x)
            step(x + offset)
        return run

    loop(1, 5, both(lambda x: sweep(ubuf, vbuf, x), 10))
    loop(2, 6, both(lambda x: sweep(vbuf, wbuf, x), 8))
    loop(4, 7, both(residual, 5))

    def two_pieces(value, matrix):
        piece = value.astype(BF16)
        rest = (value - piece.astype(F32)).astype(BF16)
        product = jnp.dot(
            jnp.concatenate([piece, rest], axis=0), matrix, preferred_element_type=F32
        )
        return product[0:value.shape[0]] + product[value.shape[0]:]

    def pair_sum(p, z):
        total = None
        for x in (2 * p, 2 * p + 1):
            for r in (0, 1):
                part = rbuf[x, z, pl.ds(r, 16, stride=2), :]
                total = part if total is None else total + part
        return total

    lane_pairs = jnp.where(lax.div(iota((256, 128), 0), 2) == iota((256, 128), 1), 0.5, 0.0)
    lane_pairs = lane_pairs.astype(BF16)
    for h in range(2):
        sums = jnp.concatenate(
            [
                jnp.concatenate([pair_sum(p, 2 * h), pair_sum(p, 2 * h + 1)], axis=1)
                for p in range(4)
            ],
            axis=0,
        )
        coarse_target = two_pieces(sums, lane_pairs)
        at_h = slice(h * 128, (h + 1) * 128)
        for p in range(4):
            plane = coarse_target[p * 16:(p + 1) * 16]
            rounded = plane.astype(BF16)
            cb[p, :, at_h] = rounded
            cb_low[p, :, at_h] = rounded[0:4]
            cb_high[p, :, at_h] = rounded[12:16]
            cbuf[4 + p, h, 12:28, :] = plane
    third = exchange(
        2,
        [cb, cb, cb_high, cb_low, cb_high, cb_low, cb_high, cb_low],
        [xc_low, xc_high, yc_low.at[pl.ds(4, 4)], yc_high.at[pl.ds(4, 4)],
         yc_low.at[pl.ds(0, 4)], yc_high.at[pl.ds(0, 4)],
         yc_low.at[pl.ds(8, 4)], yc_high.at[pl.ds(8, 4)]],
    )
    blocks += [send_block(k) for k in (2, 6, 1, 7)]
    moved = []
    for i, step in enumerate((1, -1)):
        copy = pltpu.make_async_remote_copy(
            src_ref=movers.at[i],
            dst_ref=spec_out.at[pl.ds(n_depth * CAP + i * MIG, MIG), :],
            send_sem=mig_send.at[i],
            recv_sem=mig_recv.at[i],
            device_id=at(step, 0),
            device_id_type=MESH,
        )
        copy.start()
        moved.append(copy)
    for copy in third:
        copy.wait_recv()

    for p in range(12):
        low = jnp.where(has_low, yc_low[p].astype(F32), 0.0)
        high = jnp.where(has_high, yc_high[p].astype(F32), 0.0)
        for h in range(2):
            at_h = slice(h * 128, (h + 1) * 128)
            if p < 4:
                cbuf[p, h, 12:28, :] = xc_low[p, :, at_h].astype(F32)
            if p >= 8:
                cbuf[p, h, 12:28, :] = xc_high[p - 8, :, at_h].astype(F32)
            cbuf[p, h, 8:12, :] = low[:, at_h]
            cbuf[p, h, 28:32, :] = high[:, at_h]
    for p in range(12):
        for h in range(2):
            dbuf[p, h, 8:32, :] = (DAMPING / COARSE_CENTRE) * cbuf[p, h, 8:32, :]

    def coarse_sweep(source_ref, target_ref, p):
        for h, (value, around) in enumerate(
            tile_sweep(source_ref, p, 2, 8, 24, first_lane, last_lane)
        ):
            result = value * (1.0 - DAMPING) + (DAMPING / COARSE_CENTRE) * (
                cbuf[p, h, 8:32, :] + around
            )
            target_ref[p, h, 8:32, :] = masked(result, 24)

    loop(1, 6, both(lambda p: coarse_sweep(dbuf, ebuf, p), 5))
    loop(2, 6, both(lambda p: coarse_sweep(ebuf, dbuf, p), 4))
    loop(3, 6, both(lambda p: coarse_sweep(dbuf, ebuf, p), 3))

    repeat_lanes = jnp.where(iota((128, 256), 0) == lax.div(iota((128, 256), 1), 2), 1.0, 0.0)
    repeat_lanes = repeat_lanes.astype(BF16)
    for h in range(2):
        spread = two_pieces(
            jnp.concatenate([ebuf[3 + p, h, 10:34, :] for p in range(6)], axis=0), repeat_lanes
        )
        for p in range(6):
            for z in range(2):
                part = spread[p * 24:(p + 1) * 24, z * 128:(z + 1) * 128]
                sbuf[p, 2 * h + z, pl.ds(0, 24, stride=2), :] = part
                sbuf[p, 2 * h + z, pl.ds(1, 24, stride=2), :] = part

    def correct(p):
        for z in range(4):
            addition = sbuf[p, z, 0:40, :]
            for x in (2 + 2 * p, 3 + 2 * p):
                ubuf[x, z, 8:48, :] = wbuf[x, z, 8:48, :] + addition

    loop(0, 6, correct)
    loop(3, 8, both(lambda x: sweep(ubuf, vbuf, x), 5))

    def last_sweep(x):
        for z, (value, around) in enumerate(
            tile_sweep(vbuf, x, 4, 12, 32, first_lane, last_lane)
        ):
            grid_out[x - 4, :, z * 128:(z + 1) * 128] = value * (1.0 - DAMPING) + (
                DAMPING / CENTRE
            ) * (tbuf[x, z, 12:44, :] + around)

    loop(4, 8, both(last_sweep, 4))

    for copy in blocks + moved:
        copy.wait_recv()
    for copy in first + second + third + blocks + moved:
        copy.wait_send()


def local(n_slab, n_depth, nutrient, species, agent_cell, death_flag, divide_flag, slab_move,
          depth_route, net_weight, sensing, uptake_weight):
    row = (1, ROWS)
    vmem = pl.BlockSpec(memory_space=pltpu.VMEM)
    scratch = [
        ((8, 32, 512), F32), ((ROWS, WIDTH), BF16), (row, I32), (row, I32), (row, I32), (row, I32),
        (row, I32), ((WIDTH, WIDTH), BF16), ((1, WIDTH), F32), ((1, WIDTH), BF16),
        ((8, 32, 512), BF16), ((8, 4, 512), BF16), ((8, 4, 512), BF16),
        ((8, 32, 512), BF16), ((8, 4, 512), BF16), ((8, 4, 512), BF16),
        ((4, 16, 256), BF16), ((4, 4, 256), BF16), ((4, 4, 256), BF16),
        ((4, 32, 512), BF16), ((4, 32, 512), BF16), ((16, 4, 512), BF16), ((16, 4, 512), BF16),
        ((4, 32, 512), BF16), ((4, 32, 512), BF16), ((16, 4, 512), BF16), ((16, 4, 512), BF16),
        ((4, 16, 256), BF16), ((4, 16, 256), BF16), ((12, 4, 256), BF16), ((12, 4, 256), BF16),
        ((512, ROWS), BF16), ((ROWS, WIDTH), BF16), ((n_depth, CAP, WIDTH), BF16),
        ((2, MIG, WIDTH), BF16), ((6, 4, 48, 128), F32),
        ((16, 4, 56, 128), F32), ((16, 4, 56, 128), F32), ((16, 4, 56, 128), F32),
        ((16, 4, 56, 128), F32), ((8, 4, 32, 128), F32),
        ((12, 2, 40, 128), F32), ((12, 2, 40, 128), F32), ((12, 2, 40, 128), F32),
    ]
    return pl.pallas_call(
        functools.partial(kernel, n_slab, n_depth),
        out_shape=(
            jax.ShapeDtypeStruct((8, 32, 512), F32),
            jax.ShapeDtypeStruct((n_depth * CAP + 2 * MIG, WIDTH), BF16),
        ),
        in_specs=[pl.BlockSpec(memory_space=pltpu.HBM)] * 10,
        out_specs=(vmem, vmem),
        scratch_shapes=[pltpu.VMEM(shape, dtype) for shape, dtype in scratch] + [
            pltpu.SemaphoreType.DMA((3, 8)), pltpu.SemaphoreType.DMA((3, 8)),
            pltpu.SemaphoreType.DMA((n_depth,)), pltpu.SemaphoreType.DMA((n_depth,)),
            pltpu.SemaphoreType.DMA((2,)), pltpu.SemaphoreType.DMA((2,)),
            pltpu.SemaphoreType.DMA((10,)),
        ],
        compiler_params=pltpu.CompilerParams(
            collective_id=0, has_side_effects=True, vmem_limit_bytes=48 * 1024 * 1024
        ),
        name="step",
    )(
        *[pltpu.with_memory_space_constraint(v, pltpu.HBM) for v in (nutrient, species, agent_cell.reshape(row), death_flag.reshape(row),
        divide_flag.reshape(row), slab_move.reshape(row), depth_route.reshape(row),
        net_weight, sensing.reshape(1, WIDTH), uptake_weight.reshape(1, WIDTH))],
    )


def solution(mesh):
    in_specs = (
        P("slab", "depth", None),
        P(("slab", "depth"), None),
        P(("slab", "depth")),
        P(("slab", "depth")),
        P(("slab", "depth")),
        P(("slab", "depth")),
        P(("slab", "depth"), None),
        P(),
        P(),
        P(),
    )
    out_specs = (P("slab", "depth", None), P(("slab", "depth"), None))
    body = functools.partial(local, mesh.shape["slab"], mesh.shape["depth"])
    return jax.shard_map(body, mesh=mesh, in_specs=in_specs, out_specs=out_specs, check_vma=False)
```

```python
import functools

import jax
import jax.numpy as jnp
from jax import lax
from jax.experimental import pallas as pl
from jax.experimental.pallas import tpu as pltpu
from jax.sharding import PartitionSpec as P

SCREENING = 0.05
DAMPING = 2.0 / 3.0
CENTRE = 6.0 + SCREENING
COARSE_CENTRE = 6.0 + 4.0 * SCREENING
F32 = jnp.float32
BF16 = jnp.bfloat16
I32 = jnp.int32
MESH = pl.DeviceIdType.MESH

ROWS = 1024
CAP = 256
MIG = 128
WIDTH = 128
SIDES = ((1, 0), (-1, 0), (0, 1), (0, -1), (1, 1), (1, -1), (-1, 1), (-1, -1))
ORDER = (4, 5, 6, 7, 0, 1, 2, 3)


def iota(shape, axis, dtype=I32):
    values = lax.broadcasted_iota(I32, shape, axis)
    return values if dtype == I32 else values.astype(dtype)


def tile_sweep(ref, x, tiles, first_row, rows, first_lane, last_lane):
    centre = [ref[x, z, pl.ds(first_row, rows), :] for z in range(tiles)]
    before_first = jnp.where(first_lane, 0.0, pltpu.roll(centre[-1], 1, 1))
    after_last = jnp.where(last_lane, 0.0, pltpu.roll(centre[0], 127, 1))
    out = []
    for z in range(tiles):
        total = centre[z - 1] if z > 0 else before_first
        total = total + (centre[z + 1] if z < tiles - 1 else after_last)
        total = total + ref[x, z, pl.ds(first_row - 1, rows), :]
        total = total + ref[x, z, pl.ds(first_row + 1, rows), :]
        total = total + ref[x - 1, z, pl.ds(first_row, rows), :]
        total = total + ref[x + 1, z, pl.ds(first_row, rows), :]
        out.append((centre[z], total))
    return out


def kernel(
    n_slab, n_depth,
    nut_in, spec_in, cell_in, death_in, divide_in, move_in, route_in, netw_in, sensing_in, uw_in,
    grid_out, spec_out, order,
    own_nb, nut, spec, cell, death, divide, move, route, netw, sensing, uw,
    nb, nb_low, nb_high, src, src_low, src_high, cb, cb_low, cb_high,
    xr_low, xr_high, yr_low, yr_high,
    xs_low, xs_high, ys_low, ys_high,
    xc_low, xc_high, yc_low, yc_high,
    lane_hot, cell_hot, upd, packed, movers, sbuf, tbuf, ubuf, vbuf, wbuf, rbuf, cbuf, dbuf, ebuf,
    halo_send, halo_recv, a2a_send, a2a_recv, mig_send, mig_recv, in_sem,
):
    s = lax.axis_index("slab")
    d = lax.axis_index("depth")

    def at(step_s, step_d):
        return (lax.rem(s + step_s + n_slab, n_slab), lax.rem(d + step_d + n_depth, n_depth))

    barrier = pltpu.get_barrier_semaphore()
    partners = [at(a, b) for a, b in SIDES if a != 0] + [at(0, k) for k in range(1, n_depth)]
    for partner in partners:
        pl.semaphore_signal(barrier, inc=1, device_id=partner, device_id_type=MESH)

    loads = []
    for i, (source_ref, target_ref) in enumerate((
        (cell_in, cell), (nut_in, nut), (spec_in, spec), (uw_in, uw), (death_in, death),
        (divide_in, divide), (move_in, move), (route_in, route), (netw_in, netw),
        (sensing_in, sensing),
    )):
        load = pltpu.make_async_copy(source_ref, target_ref, in_sem.at[i])
        load.start()
        loads.append(load)

    def exchange(number, sources, targets):
        copies = {}
        for i in ORDER:
            a, b = SIDES[i]
            copy = pltpu.make_async_remote_copy(
                src_ref=sources[i],
                dst_ref=targets[i],
                send_sem=halo_send.at[number, i],
                recv_sem=halo_recv.at[number, i],
                device_id=at(a, b),
                device_id_type=MESH,
            )
            copy.start()
            copies[i] = copy
        return [copies[i] for i in range(len(SIDES))]

    loads[0].wait()
    cell_row = cell[...]
    z_row = lax.rem(cell_row, 512)
    xy_row = lax.div(cell_row, 512)
    place_row = lax.rem(z_row, 4) * 128 + lax.div(z_row, 4)
    places = iota((1, 512), 1)
    cell_of_place = lax.rem(places, 128) * 4 + lax.div(places, 128)

    def fill_lane(i, carry):
        start = pl.multiple_of(i * 64, 64)
        hit = iota((64, ROWS), 0) == z_row - start
        lane_hot[pl.ds(start, 64), :] = jnp.where(hit, 1.0, 0.0).astype(BF16)
        hit = iota((64, ROWS), 0) == place_row - start
        cell_hot[pl.ds(start, 64), :] = jnp.where(hit, 1.0, 0.0).astype(BF16)
        hit = iota((64, 512), 0) == cell_of_place - start
        order[pl.ds(start, 64), :] = jnp.where(hit, 1.0, 0.0).astype(BF16)
        return carry

    lax.fori_loop(0, 8, fill_lane, 0)

    loads[1].wait()
    own_nb[...] = nut[...].reshape(256, 512).astype(BF16)
    placed = jnp.dot(own_nb[...], order[...], preferred_element_type=F32).astype(BF16)
    for x in range(8):
        plane = placed[x * 32:(x + 1) * 32]
        nb[x] = plane
        nb_low[x] = plane[0:4]
        nb_high[x] = plane[28:32]
    pl.semaphore_wait(barrier, len(partners))
    first = exchange(
        0,
        [nb.at[pl.ds(4, 4)], nb.at[pl.ds(0, 4)], nb_high, nb_low,
         nb_high.at[pl.ds(5, 3)], nb_low.at[pl.ds(5, 3)],
         nb_high.at[pl.ds(0, 3)], nb_low.at[pl.ds(0, 3)]],
        [xr_low, xr_high, yr_low.at[pl.ds(4, 8)], yr_high.at[pl.ds(4, 8)],
         yr_low.at[pl.ds(1, 3)], yr_high.at[pl.ds(1, 3)],
         yr_low.at[pl.ds(12, 3)], yr_high.at[pl.ds(12, 3)]],
    )

    sampled = jnp.dot(own_nb[...], lane_hot[...], preferred_element_type=F32)
    row_hit = iota((256, ROWS), 0) == xy_row
    sample = jnp.sum(jnp.where(row_hit, sampled, 0.0), axis=0, keepdims=True)
    for load in loads[2:]:
        load.wait()
    alive = 1.0 - death[...].astype(F32)
    score = lax.dot_general(
        jnp.broadcast_to(uw[...], (16, WIDTH)), spec[...], (((1,), (1,)), ((), ())),
        preferred_element_type=F32,
    )[0:1]
    softplus = jnp.maximum(score, 0.0) + jnp.log1p(jnp.exp(-jnp.abs(score)))
    uptake = alive * (1.0 + divide[...].astype(F32)) * softplus * sample / (0.5 + sample)

    row_hit = iota((256, ROWS), 0) == xy_row
    source = lax.dot_general(
        jnp.where(row_hit, uptake, 0.0).astype(BF16), cell_hot[...], (((1,), (1,)), ((), ())),
        preferred_element_type=F32,
    ).reshape(8, 32, 512)
    for x in range(8):
        plane = source[x]
        rounded = plane.astype(BF16)
        src[x] = rounded
        src_low[x] = rounded[0:4]
        src_high[x] = rounded[28:32]
        for z in range(4):
            tbuf[4 + x, z, 12:44, :] = plane[:, z * 128:(z + 1) * 128]
    second = exchange(
        1,
        [src.at[pl.ds(5, 3)], src.at[pl.ds(0, 3)], src_high, src_low,
         src_high.at[pl.ds(6, 2)], src_low.at[pl.ds(6, 2)],
         src_high.at[pl.ds(0, 2)], src_low.at[pl.ds(0, 2)]],
        [xs_low.at[pl.ds(1, 3)], xs_high.at[pl.ds(0, 3)],
         ys_low.at[pl.ds(4, 8)], ys_high.at[pl.ds(4, 8)],
         ys_low.at[pl.ds(2, 2)], ys_high.at[pl.ds(2, 2)],
         ys_low.at[pl.ds(12, 2)], ys_high.at[pl.ds(12, 2)]],
    )
    for half in range(2):
        value = nut[4 * half:4 * half + 4].reshape(128, 512)
        rest = value - value.astype(BF16).astype(F32)
        piece = rest.astype(BF16)
        pieces = jnp.concatenate([piece, (rest - piece.astype(F32)).astype(BF16)], axis=0)
        rest = jnp.dot(pieces, order[...], preferred_element_type=F32)
        rest = rest[0:128] + rest[128:256]
        for i in range(4):
            x = 4 * half + i
            value = nb[x].astype(F32) + rest[i * 32:(i + 1) * 32]
            for z in range(4):
                part = value[:, z * 128:(z + 1) * 128]
                ubuf[4 + x, z, 12:44, :] = part
                tbuf[4 + x, z, 12:44, :] = SCREENING * part - tbuf[4 + x, z, 12:44, :]

    sensed = sample.astype(BF16).astype(F32)
    activation = jnp.dot(spec[...], netw[...], preferred_element_type=F32)
    sensed_column = jnp.transpose(jnp.broadcast_to(sensed, (WIDTH, ROWS)))
    activation = activation + sensed_column * sensing[...]
    upd[...] = (0.5 * spec[...].astype(F32) + jnp.tanh(activation)).astype(BF16)

    lanes = iota((16, ROWS), 0)
    move_row = move[...]
    route_row = route[...]
    counted = (lanes == route_row) | (lanes == 7 + move_row) & (move_row > 0)
    counted = jnp.where(counted, 1.0, 0.0)
    chosen = jnp.where(move_row == 0, route_row, 7 + move_row)
    stacked = jnp.concatenate([counted[:, a * 128:(a + 1) * 128] for a in range(8)], axis=0)
    before = jnp.where(iota((128, 128), 0) < iota((128, 128), 1), 1.0, 0.0)
    inside = jnp.dot(stacked.astype(BF16), before.astype(BF16), preferred_element_type=F32)
    total = jnp.dot(stacked.astype(BF16), jnp.ones((128, 128), BF16), preferred_element_type=F32)
    offset = jnp.zeros((16, 128), F32)
    ranks = []
    for a in range(8):
        ranks.append(inside[a * 16:(a + 1) * 16] + offset)
        offset = offset + total[a * 16:(a + 1) * 16]
    rank = jnp.concatenate(ranks, axis=1)
    rank = jnp.sum(jnp.where(lanes == chosen, rank, 0.0), axis=0, keepdims=True)
    rank = jnp.where(alive > 0.0, rank, -1.0)
    chosen = chosen.astype(F32)

    def pack(destination, slots):
        key = jnp.where(chosen == destination, rank, -1.0)
        hot = jnp.where(iota((slots, ROWS), 0, F32) == key, 1.0, 0.0).astype(BF16)
        return jnp.dot(hot, upd[...], preferred_element_type=F32).astype(BF16)

    def pack_step(k, carry):
        packed[k] = pack(lax.rem(d + k, n_depth).astype(F32), CAP)
        return carry

    lax.fori_loop(1, n_depth, pack_step, 0)
    movers[0] = pack(8.0, MIG)
    movers[1] = pack(9.0, MIG)
    own = pl.multiple_of(d * CAP, CAP)
    spec_out[pl.ds(own, CAP), :] = pack(d.astype(F32), CAP)

    def send_block(k):
        copy = pltpu.make_async_remote_copy(
            src_ref=packed.at[k],
            dst_ref=spec_out.at[pl.ds(own, CAP), :],
            send_sem=a2a_send.at[k],
            recv_sem=a2a_recv.at[k],
            device_id=at(0, k),
            device_id_type=MESH,
        )
        copy.start()
        return copy

    blocks = [send_block(k) for k in (4, 3, 5)]

    lane = iota((1, 128), 1)
    first_lane = lane == 0
    last_lane = lane == 127
    row8 = iota((8, 1), 0)
    keep_low = (row8 >= 4) | (d > 0)
    keep_high = (row8 < 4) | (d < n_depth - 1)
    has_low = jnp.full((4, 1), d, I32) > 0
    has_high = jnp.full((4, 1), d, I32) < n_depth - 1

    def fill_rows(x, with_source):
        low = jnp.where(has_low, yr_low[x].astype(F32), 0.0)
        high = jnp.where(has_high, yr_high[x].astype(F32), 0.0)
        for z in range(4):
            at_z = slice(z * 128, (z + 1) * 128)
            ubuf[x, z, 8:12, :] = low[:, at_z]
            ubuf[x, z, 44:48, :] = high[:, at_z]
        if with_source:
            low = SCREENING * low - ys_low[x].astype(F32)
            high = SCREENING * high - ys_high[x].astype(F32)
            for z in range(4):
                at_z = slice(z * 128, (z + 1) * 128)
                tbuf[x, z, 8:12, :] = low[:, at_z]
                tbuf[x, z, 44:48, :] = high[:, at_z]

    def masked(value, rows):
        return jnp.concatenate(
            [jnp.where(keep_low, value[0:8], 0.0), value[8:rows - 8],
             jnp.where(keep_high, value[rows - 8:], 0.0)], axis=0,
        )

    def sweep(source_ref, target_ref, x):
        for z, (value, around) in enumerate(
            tile_sweep(source_ref, x, 4, 8, 40, first_lane, last_lane)
        ):
            result = value * (1.0 - DAMPING) + (DAMPING / CENTRE) * (tbuf[x, z, 8:48, :] + around)
            target_ref[x, z, 8:48, :] = masked(result, 40)

    def residual(x):
        for z, (value, around) in enumerate(
            tile_sweep(wbuf, x, 4, 12, 32, first_lane, last_lane)
        ):
            rbuf[x - 4, z] = tbuf[x, z, 12:44, :] + around - CENTRE * value

    def loop(begin, end, step):
        lax.fori_loop(begin, end, lambda x, carry: (step(x), carry)[1], 0)

    for copy in (first[2], first[3], second[2], second[3]):
        copy.wait_recv()
    loop(4, 12, lambda x: fill_rows(x, True))
    loop(5, 11, lambda x: sweep(ubuf, vbuf, x))
    loop(6, 10, lambda x: sweep(vbuf, wbuf, x))
    loop(7, 9, residual)

    for i in (0, 1, 4, 5, 6, 7):
        first[i].wait_recv()
        second[i].wait_recv()

    def fill_plane(x, value, taken):
        value = value.astype(F32)
        for z in range(4):
            ubuf[x, z, 12:44, :] = value[:, z * 128:(z + 1) * 128]
        if taken is not None:
            value = SCREENING * value - taken.astype(F32)
            for z in range(4):
                tbuf[x, z, 12:44, :] = value[:, z * 128:(z + 1) * 128]
        fill_rows(x, taken is not None)

    fill_plane(0, xr_low[0], None)
    fill_plane(15, xr_high[3], None)

    def fill_outer(i):
        fill_plane(i, xr_low[i], xs_low[i])
        fill_plane(11 + i, xr_high[i - 1], xs_high[i - 1])

    loop(1, 4, fill_outer)

    def both(step, offset):
        def run(x):
            step(x)
            step(x + offset)
        return run

    loop(1, 5, both(lambda x: sweep(ubuf, vbuf, x), 10))
    loop(2, 6, both(lambda x: sweep(vbuf, wbuf, x), 8))
    loop(4, 7, both(residual, 5))

    def pair_sum(p, z):
        total = None
        for x in (2 * p, 2 * p + 1):
            for r in (0, 1):
                part = rbuf[x, z, pl.ds(r, 16, stride=2), :]
                total = part if total is None else total + part
        return total

    for h in range(2):
        at_h = slice(h * 128, (h + 1) * 128)
        for p in range(4):
            plane = 0.5 * (pair_sum(p, 2 * h) + pair_sum(p, 2 * h + 1))
            rounded = plane.astype(BF16)
            cb[p, :, at_h] = rounded
            cb_low[p, :, at_h] = rounded[0:4]
            cb_high[p, :, at_h] = rounded[12:16]
            cbuf[4 + p, h, 12:28, :] = plane
    third = exchange(
        2,
        [cb, cb, cb_high, cb_low, cb_high, cb_low, cb_high, cb_low],
        [xc_low, xc_high, yc_low.at[pl.ds(4, 4)], yc_high.at[pl.ds(4, 4)],
         yc_low.at[pl.ds(0, 4)], yc_high.at[pl.ds(0, 4)],
         yc_low.at[pl.ds(8, 4)], yc_high.at[pl.ds(8, 4)]],
    )
    blocks += [send_block(k) for k in (2, 6, 1, 7)]
    moved = []
    for i, step in enumerate((1, -1)):
        copy = pltpu.make_async_remote_copy(
            src_ref=movers.at[i],
            dst_ref=spec_out.at[pl.ds(n_depth * CAP + i * MIG, MIG), :],
            send_sem=mig_send.at[i],
            recv_sem=mig_recv.at[i],
            device_id=at(step, 0),
            device_id_type=MESH,
        )
        copy.start()
        moved.append(copy)
    for copy in third:
        copy.wait_recv()

    for p in range(12):
        low = jnp.where(has_low, yc_low[p].astype(F32), 0.0)
        high = jnp.where(has_high, yc_high[p].astype(F32), 0.0)
        for h in range(2):
            at_h = slice(h * 128, (h + 1) * 128)
            if p < 4:
                cbuf[p, h, 12:28, :] = xc_low[p, :, at_h].astype(F32)
            if p >= 8:
                cbuf[p, h, 12:28, :] = xc_high[p - 8, :, at_h].astype(F32)
            cbuf[p, h, 8:12, :] = low[:, at_h]
            cbuf[p, h, 28:32, :] = high[:, at_h]
    for p in range(12):
        for h in range(2):
            dbuf[p, h, 8:32, :] = (DAMPING / COARSE_CENTRE) * cbuf[p, h, 8:32, :]

    def coarse_sweep(source_ref, target_ref, p):
        for h, (value, around) in enumerate(
            tile_sweep(source_ref, p, 2, 8, 24, first_lane, last_lane)
        ):
            result = value * (1.0 - DAMPING) + (DAMPING / COARSE_CENTRE) * (
                cbuf[p, h, 8:32, :] + around
            )
            target_ref[p, h, 8:32, :] = masked(result, 24)

    loop(1, 6, both(lambda p: coarse_sweep(dbuf, ebuf, p), 5))
    loop(2, 6, both(lambda p: coarse_sweep(ebuf, dbuf, p), 4))
    loop(3, 6, both(lambda p: coarse_sweep(dbuf, ebuf, p), 3))

    for p in range(6):
        for h in range(2):
            part = ebuf[3 + p, h, 10:34, :]
            sbuf[p, h, pl.ds(0, 24, stride=2), :] = part
            sbuf[p, h, pl.ds(1, 24, stride=2), :] = part

    def correct(p):
        for h in range(2):
            addition = sbuf[p, h, 0:40, :]
            for x in (2 + 2 * p, 3 + 2 * p):
                for z in (2 * h, 2 * h + 1):
                    ubuf[x, z, 8:48, :] = wbuf[x, z, 8:48, :] + addition

    loop(0, 6, correct)
    loop(3, 8, both(lambda x: sweep(ubuf, vbuf, x), 5))

    def last_sweep(x):
        for z, (value, around) in enumerate(
            tile_sweep(vbuf, x, 4, 12, 32, first_lane, last_lane)
        ):
            grid_out[x - 4, :, z * 128:(z + 1) * 128] = value * (1.0 - DAMPING) + (
                DAMPING / CENTRE
            ) * (tbuf[x, z, 12:44, :] + around)

    loop(4, 8, both(last_sweep, 4))

    for copy in blocks + moved:
        copy.wait_recv()
    for copy in first + second + third + blocks + moved:
        copy.wait_send()


def finish(placed, species_next, order, grid_out, spec_out, grid, sem):
    copies = [pltpu.make_async_copy(species_next, spec_out, sem.at[0])]
    copies[0].start()
    for half in range(2):
        value = placed[4 * half:4 * half + 4].reshape(128, 512)
        piece = value.astype(BF16)
        rest = (value - piece.astype(F32)).astype(BF16)
        both = lax.dot_general(
            jnp.concatenate([piece, rest], axis=0), order[...], (((1,), (1,)), ((), ())),
            preferred_element_type=F32,
        )
        grid[4 * half:4 * half + 4] = (both[0:128] + both[128:256]).reshape(4, 32, 512)
        at_half = pl.ds(4 * half, 4)
        copies.append(pltpu.make_async_copy(grid.at[at_half], grid_out.at[at_half], sem.at[1 + half]))
        copies[-1].start()
    for copy in copies:
        copy.wait()


def local(n_slab, n_depth, nutrient, species, agent_cell, death_flag, divide_flag, slab_move,
          depth_route, net_weight, sensing, uptake_weight):
    row = (1, ROWS)
    vmem = pl.BlockSpec(memory_space=pltpu.VMEM)
    scratch = [
        ((256, 512), BF16),
        ((8, 32, 512), F32), ((ROWS, WIDTH), BF16), (row, I32), (row, I32), (row, I32), (row, I32),
        (row, I32), ((WIDTH, WIDTH), BF16), ((1, WIDTH), F32), ((1, WIDTH), BF16),
        ((8, 32, 512), BF16), ((8, 4, 512), BF16), ((8, 4, 512), BF16),
        ((8, 32, 512), BF16), ((8, 4, 512), BF16), ((8, 4, 512), BF16),
        ((4, 16, 256), BF16), ((4, 4, 256), BF16), ((4, 4, 256), BF16),
        ((4, 32, 512), BF16), ((4, 32, 512), BF16), ((16, 4, 512), BF16), ((16, 4, 512), BF16),
        ((4, 32, 512), BF16), ((4, 32, 512), BF16), ((16, 4, 512), BF16), ((16, 4, 512), BF16),
        ((4, 16, 256), BF16), ((4, 16, 256), BF16), ((12, 4, 256), BF16), ((12, 4, 256), BF16),
        ((512, ROWS), BF16), ((512, ROWS), BF16), ((ROWS, WIDTH), BF16), ((n_depth, CAP, WIDTH), BF16),
        ((2, MIG, WIDTH), BF16), ((6, 2, 48, 128), F32),
        ((16, 4, 56, 128), F32), ((16, 4, 56, 128), F32), ((16, 4, 56, 128), F32),
        ((16, 4, 56, 128), F32), ((8, 4, 32, 128), F32),
        ((12, 2, 40, 128), F32), ((12, 2, 40, 128), F32), ((12, 2, 40, 128), F32),
    ]
    placed, species_next, order = pl.pallas_call(
        functools.partial(kernel, n_slab, n_depth),
        out_shape=(
            jax.ShapeDtypeStruct((8, 32, 512), F32),
            jax.ShapeDtypeStruct((n_depth * CAP + 2 * MIG, WIDTH), BF16),
            jax.ShapeDtypeStruct((512, 512), BF16),
        ),
        in_specs=[pl.BlockSpec(memory_space=pltpu.HBM)] * 10,
        out_specs=(vmem, vmem, vmem),
        scratch_shapes=[pltpu.VMEM(shape, dtype) for shape, dtype in scratch] + [
            pltpu.SemaphoreType.DMA((3, 8)), pltpu.SemaphoreType.DMA((3, 8)),
            pltpu.SemaphoreType.DMA((n_depth,)), pltpu.SemaphoreType.DMA((n_depth,)),
            pltpu.SemaphoreType.DMA((2,)), pltpu.SemaphoreType.DMA((2,)),
            pltpu.SemaphoreType.DMA((10,)),
        ],
        compiler_params=pltpu.CompilerParams(
            collective_id=0, has_side_effects=True, vmem_limit_bytes=48 * 1024 * 1024
        ),
        name="step",
    )(
        *[pltpu.with_memory_space_constraint(v, pltpu.HBM) for v in (nutrient, species, agent_cell.reshape(row), death_flag.reshape(row),
        divide_flag.reshape(row), slab_move.reshape(row), depth_route.reshape(row),
        net_weight, sensing.reshape(1, WIDTH), uptake_weight.reshape(1, WIDTH))],
    )
    return pl.pallas_call(
        finish,
        out_shape=(
            jax.ShapeDtypeStruct((8, 32, 512), F32),
            jax.ShapeDtypeStruct((n_depth * CAP + 2 * MIG, WIDTH), BF16),
        ),
        in_specs=[vmem] * 3,
        out_specs=(pl.BlockSpec(memory_space=pl.ANY), pl.BlockSpec(memory_space=pl.ANY)),
        scratch_shapes=[pltpu.VMEM((8, 32, 512), F32), pltpu.SemaphoreType.DMA((3,))],
        compiler_params=pltpu.CompilerParams(vmem_limit_bytes=16 * 1024 * 1024),
        name="finish",
    )(placed, species_next, order)


def solution(mesh):
    in_specs = (
        P("slab", "depth", None),
        P(("slab", "depth"), None),
        P(("slab", "depth")),
        P(("slab", "depth")),
        P(("slab", "depth")),
        P(("slab", "depth")),
        P(("slab", "depth"), None),
        P(),
        P(),
        P(),
    )
    out_specs = (P("slab", "depth", None), P(("slab", "depth"), None))
    body = functools.partial(local, mesh.shape["slab"], mesh.shape["depth"])
    return jax.shard_map(body, mesh=mesh, in_specs=in_specs, out_specs=out_specs, check_vma=False)
```

```python
import functools

import jax
import jax.numpy as jnp
from jax import lax
from jax.experimental import pallas as pl
from jax.experimental.pallas import tpu as pltpu
from jax.sharding import PartitionSpec as P

SCREENING = 0.05
DAMPING = 2.0 / 3.0
CENTRE = 6.0 + SCREENING
COARSE_CENTRE = 6.0 + 4.0 * SCREENING
F32 = jnp.float32
BF16 = jnp.bfloat16
I32 = jnp.int32
MESH = pl.DeviceIdType.MESH

ROWS = 1024
CAP = 256
MIG = 128
WIDTH = 128
SIDES = ((1, 0), (-1, 0), (0, 1), (0, -1), (1, 1), (1, -1), (-1, 1), (-1, -1))
ORDER = (4, 5, 6, 7, 0, 1, 2, 3)


def iota(shape, axis, dtype=I32):
    values = lax.broadcasted_iota(I32, shape, axis)
    return values if dtype == I32 else values.astype(dtype)


def tile_sweep(ref, x, tiles, first_row, rows, first_lane, last_lane):
    centre = [ref[x, z, pl.ds(first_row, rows), :] for z in range(tiles)]
    before_first = jnp.where(first_lane, 0.0, pltpu.roll(centre[-1], 1, 1))
    after_last = jnp.where(last_lane, 0.0, pltpu.roll(centre[0], 127, 1))
    out = []
    for z in range(tiles):
        total = centre[z - 1] if z > 0 else before_first
        total = total + (centre[z + 1] if z < tiles - 1 else after_last)
        total = total + ref[x, z, pl.ds(first_row - 1, rows), :]
        total = total + ref[x, z, pl.ds(first_row + 1, rows), :]
        total = total + ref[x - 1, z, pl.ds(first_row, rows), :]
        total = total + ref[x + 1, z, pl.ds(first_row, rows), :]
        out.append((centre[z], total))
    return out


def kernel(
    n_slab, n_depth,
    nut_in, spec_in, cell_in, death_in, divide_in, move_in, route_in, netw_in, sensing_in, uw_in,
    grid_out, spec_out, order,
    own_nb, nut, spec, cell, death, divide, move, route, netw, sensing, uw,
    nb, nb_low, nb_high, src, src_low, src_high, cb, cb_low, cb_high,
    xr_low, xr_high, yr_low, yr_high,
    xs_low, xs_high, ys_low, ys_high,
    xc_low, xc_high, yc_low, yc_high,
    lane_hot, cell_hot, upd, packed, movers, sbuf, tbuf, ubuf, vbuf, wbuf, rbuf, cbuf, dbuf, ebuf,
    sampled_row, halo_send, halo_recv, a2a_send, a2a_recv, mig_send, mig_recv, in_sem,
):
    s = lax.axis_index("slab")
    d = lax.axis_index("depth")

    def at(step_s, step_d):
        return (lax.rem(s + step_s + n_slab, n_slab), lax.rem(d + step_d + n_depth, n_depth))

    barrier = pltpu.get_barrier_semaphore()
    partners = [at(a, b) for a, b in SIDES if a != 0] + [at(0, k) for k in range(1, n_depth)]
    for partner in partners:
        pl.semaphore_signal(barrier, inc=1, device_id=partner, device_id_type=MESH)

    loads = []
    for i, (source_ref, target_ref) in enumerate((
        (cell_in, cell), (nut_in, nut), (spec_in, spec), (uw_in, uw), (death_in, death),
        (divide_in, divide), (move_in, move), (route_in, route), (netw_in, netw),
        (sensing_in, sensing),
    )):
        load = pltpu.make_async_copy(source_ref, target_ref, in_sem.at[i])
        load.start()
        loads.append(load)

    def exchange(number, sources, targets):
        copies = {}
        for i in ORDER:
            a, b = SIDES[i]
            copy = pltpu.make_async_remote_copy(
                src_ref=sources[i],
                dst_ref=targets[i],
                send_sem=halo_send.at[number, i],
                recv_sem=halo_recv.at[number, i],
                device_id=at(a, b),
                device_id_type=MESH,
            )
            copy.start()
            copies[i] = copy
        return [copies[i] for i in range(len(SIDES))]

    loads[0].wait()
    cell_row = cell[...]
    z_row = lax.rem(cell_row, 512)
    xy_row = lax.div(cell_row, 512)
    place_row = lax.rem(z_row, 4) * 128 + lax.div(z_row, 4)
    places = iota((1, 512), 1)
    cell_of_place = lax.rem(places, 128) * 4 + lax.div(places, 128)

    def fill_lane(i, carry):
        start = pl.multiple_of(i * 64, 64)
        hit = iota((64, ROWS), 0) == z_row - start
        lane_hot[pl.ds(start, 64), :] = jnp.where(hit, 1.0, 0.0).astype(BF16)
        hit = iota((64, ROWS), 0) == place_row - start
        cell_hot[pl.ds(start, 64), :] = jnp.where(hit, 1.0, 0.0).astype(BF16)
        hit = iota((64, 512), 0) == cell_of_place - start
        order[pl.ds(start, 64), :] = jnp.where(hit, 1.0, 0.0).astype(BF16)
        return carry

    lax.fori_loop(0, 8, fill_lane, 0)

    loads[1].wait()
    own_nb[...] = nut[...].reshape(256, 512).astype(BF16)
    placed = jnp.dot(own_nb[...], order[...], preferred_element_type=F32).astype(BF16)
    for x in range(8):
        plane = placed[x * 32:(x + 1) * 32]
        nb[x] = plane
        nb_low[x] = plane[0:4]
        nb_high[x] = plane[28:32]
    for load in loads[2:]:
        load.wait()
    own = pl.multiple_of(d * CAP, CAP)

    def gather_and_scatter():
        sampled = jnp.dot(own_nb[...], lane_hot[...], preferred_element_type=F32)
        row_hit = iota((256, ROWS), 0) == xy_row
        sample = jnp.sum(jnp.where(row_hit, sampled, 0.0), axis=0, keepdims=True)
        sampled_row[...] = sample
        alive = 1.0 - death[...].astype(F32)
        score = lax.dot_general(
            jnp.broadcast_to(uw[...], (16, WIDTH)), spec[...], (((1,), (1,)), ((), ())),
            preferred_element_type=F32,
        )[0:1]
        softplus = jnp.maximum(score, 0.0) + jnp.log1p(jnp.exp(-jnp.abs(score)))
        uptake = alive * (1.0 + divide[...].astype(F32)) * softplus * sample / (0.5 + sample)

        row_hit = iota((256, ROWS), 0) == xy_row
        source = lax.dot_general(
            jnp.where(row_hit, uptake, 0.0).astype(BF16), cell_hot[...], (((1,), (1,)), ((), ())),
            preferred_element_type=F32,
        ).reshape(8, 32, 512)
        for x in range(8):
            plane = source[x]
            rounded = plane.astype(BF16)
            src[x] = rounded
            src_low[x] = rounded[0:4]
            src_high[x] = rounded[28:32]
            for z in range(4):
                tbuf[4 + x, z, 12:44, :] = plane[:, z * 128:(z + 1) * 128]

    def species_work():
        sensed = sampled_row[...].astype(BF16).astype(F32)
        activation = jnp.dot(spec[...], netw[...], preferred_element_type=F32)
        sensed_column = jnp.transpose(jnp.broadcast_to(sensed, (WIDTH, ROWS)))
        activation = activation + sensed_column * sensing[...]
        upd[...] = (0.5 * spec[...].astype(F32) + jnp.tanh(activation)).astype(BF16)

        lanes = iota((16, ROWS), 0)
        move_row = move[...]
        route_row = route[...]
        counted = (lanes == route_row) | (lanes == 7 + move_row) & (move_row > 0)
        counted = jnp.where(counted, 1.0, 0.0)
        chosen = jnp.where(move_row == 0, route_row, 7 + move_row)
        stacked = jnp.concatenate([counted[:, a * 128:(a + 1) * 128] for a in range(8)], axis=0)
        before = jnp.where(iota((128, 128), 0) < iota((128, 128), 1), 1.0, 0.0)
        inside = jnp.dot(stacked.astype(BF16), before.astype(BF16), preferred_element_type=F32)
        total = jnp.dot(stacked.astype(BF16), jnp.ones((128, 128), BF16), preferred_element_type=F32)
        offset = jnp.zeros((16, 128), F32)
        ranks = []
        for a in range(8):
            ranks.append(inside[a * 16:(a + 1) * 16] + offset)
            offset = offset + total[a * 16:(a + 1) * 16]
        rank = jnp.concatenate(ranks, axis=1)
        rank = jnp.sum(jnp.where(lanes == chosen, rank, 0.0), axis=0, keepdims=True)
        rank = jnp.where(death[...] == 0, rank, -1.0)
        chosen = chosen.astype(F32)

        def pack(destination, slots):
            key = jnp.where(chosen == destination, rank, -1.0)
            hot = jnp.where(iota((slots, ROWS), 0, F32) == key, 1.0, 0.0).astype(BF16)
            return jnp.dot(hot, upd[...], preferred_element_type=F32).astype(BF16)

        def pack_step(k, carry):
            packed[k] = pack(lax.rem(d + k, n_depth).astype(F32), CAP)
            return carry

        lax.fori_loop(1, n_depth, pack_step, 0)
        movers[0] = pack(8.0, MIG)
        movers[1] = pack(9.0, MIG)
        spec_out[pl.ds(own, CAP), :] = pack(d.astype(F32), CAP)

    early = s == 0
    later = s > 0
    pl.when(early)(gather_and_scatter)
    pl.when(early & (d > 0))(species_work)

    pl.semaphore_wait(barrier, len(partners))
    first = exchange(
        0,
        [nb.at[pl.ds(4, 4)], nb.at[pl.ds(0, 4)], nb_high, nb_low,
         nb_high.at[pl.ds(5, 3)], nb_low.at[pl.ds(5, 3)],
         nb_high.at[pl.ds(0, 3)], nb_low.at[pl.ds(0, 3)]],
        [xr_low, xr_high, yr_low.at[pl.ds(4, 8)], yr_high.at[pl.ds(4, 8)],
         yr_low.at[pl.ds(1, 3)], yr_high.at[pl.ds(1, 3)],
         yr_low.at[pl.ds(12, 3)], yr_high.at[pl.ds(12, 3)]],
    )

    pl.when(later)(gather_and_scatter)
    second = exchange(
        1,
        [src.at[pl.ds(5, 3)], src.at[pl.ds(0, 3)], src_high, src_low,
         src_high.at[pl.ds(6, 2)], src_low.at[pl.ds(6, 2)],
         src_high.at[pl.ds(0, 2)], src_low.at[pl.ds(0, 2)]],
        [xs_low.at[pl.ds(1, 3)], xs_high.at[pl.ds(0, 3)],
         ys_low.at[pl.ds(4, 8)], ys_high.at[pl.ds(4, 8)],
         ys_low.at[pl.ds(2, 2)], ys_high.at[pl.ds(2, 2)],
         ys_low.at[pl.ds(12, 2)], ys_high.at[pl.ds(12, 2)]],
    )
    for half in range(2):
        value = nut[4 * half:4 * half + 4].reshape(128, 512)
        rest = value - value.astype(BF16).astype(F32)
        piece = rest.astype(BF16)
        pieces = jnp.concatenate([piece, (rest - piece.astype(F32)).astype(BF16)], axis=0)
        rest = jnp.dot(pieces, order[...], preferred_element_type=F32)
        rest = rest[0:128] + rest[128:256]
        for i in range(4):
            x = 4 * half + i
            value = nb[x].astype(F32) + rest[i * 32:(i + 1) * 32]
            for z in range(4):
                part = value[:, z * 128:(z + 1) * 128]
                ubuf[4 + x, z, 12:44, :] = part
                tbuf[4 + x, z, 12:44, :] = SCREENING * part - tbuf[4 + x, z, 12:44, :]

    pl.when(later | (d == 0))(species_work)

    def send_block(k):
        return pltpu.make_async_remote_copy(
            src_ref=packed.at[k],
            dst_ref=spec_out.at[pl.ds(own, CAP), :],
            send_sem=a2a_send.at[k],
            recv_sem=a2a_recv.at[k],
            device_id=at(0, k),
            device_id_type=MESH,
        )

    blocks = [send_block(k) for k in (4, 3, 5, 2, 6, 1, 7)]

    def start_rest():
        for copy in blocks[3:]:
            copy.start()

    for copy in blocks[:3]:
        copy.start()
    pl.when(s < 4)(start_rest)

    lane = iota((1, 128), 1)
    first_lane = lane == 0
    last_lane = lane == 127
    row8 = iota((8, 1), 0)
    keep_low = (row8 >= 4) | (d > 0)
    keep_high = (row8 < 4) | (d < n_depth - 1)
    has_low = jnp.full((4, 1), d, I32) > 0
    has_high = jnp.full((4, 1), d, I32) < n_depth - 1

    def fill_rows(x, with_source):
        low = jnp.where(has_low, yr_low[x].astype(F32), 0.0)
        high = jnp.where(has_high, yr_high[x].astype(F32), 0.0)
        for z in range(4):
            at_z = slice(z * 128, (z + 1) * 128)
            ubuf[x, z, 8:12, :] = low[:, at_z]
            ubuf[x, z, 44:48, :] = high[:, at_z]
        if with_source:
            low = SCREENING * low - ys_low[x].astype(F32)
            high = SCREENING * high - ys_high[x].astype(F32)
            for z in range(4):
                at_z = slice(z * 128, (z + 1) * 128)
                tbuf[x, z, 8:12, :] = low[:, at_z]
                tbuf[x, z, 44:48, :] = high[:, at_z]

    def masked(value, rows):
        return jnp.concatenate(
            [jnp.where(keep_low, value[0:8], 0.0), value[8:rows - 8],
             jnp.where(keep_high, value[rows - 8:], 0.0)], axis=0,
        )

    def sweep(source_ref, target_ref, x):
        for z, (value, around) in enumerate(
            tile_sweep(source_ref, x, 4, 8, 40, first_lane, last_lane)
        ):
            result = value * (1.0 - DAMPING) + (DAMPING / CENTRE) * (tbuf[x, z, 8:48, :] + around)
            target_ref[x, z, 8:48, :] = masked(result, 40)

    def residual(x):
        for z, (value, around) in enumerate(
            tile_sweep(wbuf, x, 4, 12, 32, first_lane, last_lane)
        ):
            rbuf[x - 4, z] = tbuf[x, z, 12:44, :] + around - CENTRE * value

    def loop(begin, end, step):
        lax.fori_loop(begin, end, lambda x, carry: (step(x), carry)[1], 0)

    for copy in (first[2], first[3], second[2], second[3]):
        copy.wait_recv()
    loop(4, 12, lambda x: fill_rows(x, True))
    loop(5, 11, lambda x: sweep(ubuf, vbuf, x))
    loop(6, 10, lambda x: sweep(vbuf, wbuf, x))
    loop(7, 9, residual)

    def fill_plane(x, value, taken):
        value = value.astype(F32)
        for z in range(4):
            ubuf[x, z, 12:44, :] = value[:, z * 128:(z + 1) * 128]
        if taken is not None:
            value = SCREENING * value - taken.astype(F32)
            for z in range(4):
                tbuf[x, z, 12:44, :] = value[:, z * 128:(z + 1) * 128]
        fill_rows(x, taken is not None)

    def both(step, offset):
        def run(x):
            step(x)
            step(x + offset)
        return run

    def low_side():
        for i in (0, 4, 5):
            first[i].wait_recv()
            second[i].wait_recv()
        fill_plane(0, xr_low[0], None)
        for i in range(1, 4):
            fill_plane(i, xr_low[i], xs_low[i])
        loop(1, 3, both(lambda x: sweep(ubuf, vbuf, x), 2))
        loop(2, 4, both(lambda x: sweep(vbuf, wbuf, x), 2))
        loop(4, 7, residual)

    def high_side():
        for i in (1, 6, 7):
            first[i].wait_recv()
            second[i].wait_recv()
        fill_plane(15, xr_high[3], None)
        for i in range(0, 3):
            fill_plane(12 + i, xr_high[i], xs_high[i])
        loop(11, 13, both(lambda x: sweep(ubuf, vbuf, x), 2))
        loop(10, 12, both(lambda x: sweep(vbuf, wbuf, x), 2))
        loop(9, 12, residual)

    @pl.when(s == n_slab - 1)
    def _():
        low_side()
        high_side()

    @pl.when(s < n_slab - 1)
    def _():
        high_side()
        low_side()

    def pair_sum(p, z):
        total = None
        for x in (2 * p, 2 * p + 1):
            for r in (0, 1):
                part = rbuf[x, z, pl.ds(r, 16, stride=2), :]
                total = part if total is None else total + part
        return total

    for h in range(2):
        at_h = slice(h * 128, (h + 1) * 128)
        for p in range(4):
            plane = 0.5 * (pair_sum(p, 2 * h) + pair_sum(p, 2 * h + 1))
            rounded = plane.astype(BF16)
            cb[p, :, at_h] = rounded
            cb_low[p, :, at_h] = rounded[0:4]
            cb_high[p, :, at_h] = rounded[12:16]
            cbuf[4 + p, h, 12:28, :] = plane
    third = exchange(
        2,
        [cb, cb, cb_high, cb_low, cb_high, cb_low, cb_high, cb_low],
        [xc_low, xc_high, yc_low.at[pl.ds(4, 4)], yc_high.at[pl.ds(4, 4)],
         yc_low.at[pl.ds(0, 4)], yc_high.at[pl.ds(0, 4)],
         yc_low.at[pl.ds(8, 4)], yc_high.at[pl.ds(8, 4)]],
    )
    pl.when(s >= 4)(start_rest)
    moved = []
    for i, step in enumerate((1, -1)):
        copy = pltpu.make_async_remote_copy(
            src_ref=movers.at[i],
            dst_ref=spec_out.at[pl.ds(n_depth * CAP + i * MIG, MIG), :],
            send_sem=mig_send.at[i],
            recv_sem=mig_recv.at[i],
            device_id=at(step, 0),
            device_id_type=MESH,
        )
        copy.start()
        moved.append(copy)
    for copy in third:
        copy.wait_recv()

    for p in range(12):
        low = jnp.where(has_low, yc_low[p].astype(F32), 0.0)
        high = jnp.where(has_high, yc_high[p].astype(F32), 0.0)
        for h in range(2):
            at_h = slice(h * 128, (h + 1) * 128)
            if p < 4:
                cbuf[p, h, 12:28, :] = xc_low[p, :, at_h].astype(F32)
            if p >= 8:
                cbuf[p, h, 12:28, :] = xc_high[p - 8, :, at_h].astype(F32)
            cbuf[p, h, 8:12, :] = low[:, at_h]
            cbuf[p, h, 28:32, :] = high[:, at_h]
    for p in range(12):
        for h in range(2):
            dbuf[p, h, 8:32, :] = (DAMPING / COARSE_CENTRE) * cbuf[p, h, 8:32, :]

    def coarse_sweep(source_ref, target_ref, p):
        for h, (value, around) in enumerate(
            tile_sweep(source_ref, p, 2, 8, 24, first_lane, last_lane)
        ):
            result = value * (1.0 - DAMPING) + (DAMPING / COARSE_CENTRE) * (
                cbuf[p, h, 8:32, :] + around
            )
            target_ref[p, h, 8:32, :] = masked(result, 24)

    loop(1, 6, both(lambda p: coarse_sweep(dbuf, ebuf, p), 5))
    loop(2, 6, both(lambda p: coarse_sweep(ebuf, dbuf, p), 4))
    loop(3, 6, both(lambda p: coarse_sweep(dbuf, ebuf, p), 3))

    for p in range(6):
        for h in range(2):
            part = ebuf[3 + p, h, 10:34, :]
            sbuf[p, h, pl.ds(0, 24, stride=2), :] = part
            sbuf[p, h, pl.ds(1, 24, stride=2), :] = part

    def correct(p):
        for h in range(2):
            addition = sbuf[p, h, 0:40, :]
            for x in (2 + 2 * p, 3 + 2 * p):
                for z in (2 * h, 2 * h + 1):
                    ubuf[x, z, 8:48, :] = wbuf[x, z, 8:48, :] + addition

    loop(0, 6, correct)
    loop(3, 8, both(lambda x: sweep(ubuf, vbuf, x), 5))

    def last_sweep(x):
        for z, (value, around) in enumerate(
            tile_sweep(vbuf, x, 4, 12, 32, first_lane, last_lane)
        ):
            grid_out[x - 4, :, z * 128:(z + 1) * 128] = value * (1.0 - DAMPING) + (
                DAMPING / CENTRE
            ) * (tbuf[x, z, 12:44, :] + around)

    loop(4, 8, both(last_sweep, 4))

    for copy in blocks + moved:
        copy.wait_recv()
    for copy in first + second + third + blocks + moved:
        copy.wait_send()


def finish(placed, species_next, order, grid_out, spec_out, grid, sem):
    copies = [pltpu.make_async_copy(species_next, spec_out, sem.at[0])]
    copies[0].start()
    for half in range(2):
        value = placed[4 * half:4 * half + 4].reshape(128, 512)
        piece = value.astype(BF16)
        rest = (value - piece.astype(F32)).astype(BF16)
        both = lax.dot_general(
            jnp.concatenate([piece, rest], axis=0), order[...], (((1,), (1,)), ((), ())),
            preferred_element_type=F32,
        )
        grid[4 * half:4 * half + 4] = (both[0:128] + both[128:256]).reshape(4, 32, 512)
        at_half = pl.ds(4 * half, 4)
        copies.append(pltpu.make_async_copy(grid.at[at_half], grid_out.at[at_half], sem.at[1 + half]))
        copies[-1].start()
    for copy in copies:
        copy.wait()


def local(n_slab, n_depth, nutrient, species, agent_cell, death_flag, divide_flag, slab_move,
          depth_route, net_weight, sensing, uptake_weight):
    row = (1, ROWS)
    vmem = pl.BlockSpec(memory_space=pltpu.VMEM)
    scratch = [
        ((256, 512), BF16),
        ((8, 32, 512), F32), ((ROWS, WIDTH), BF16), (row, I32), (row, I32), (row, I32), (row, I32),
        (row, I32), ((WIDTH, WIDTH), BF16), ((1, WIDTH), F32), ((1, WIDTH), BF16),
        ((8, 32, 512), BF16), ((8, 4, 512), BF16), ((8, 4, 512), BF16),
        ((8, 32, 512), BF16), ((8, 4, 512), BF16), ((8, 4, 512), BF16),
        ((4, 16, 256), BF16), ((4, 4, 256), BF16), ((4, 4, 256), BF16),
        ((4, 32, 512), BF16), ((4, 32, 512), BF16), ((16, 4, 512), BF16), ((16, 4, 512), BF16),
        ((4, 32, 512), BF16), ((4, 32, 512), BF16), ((16, 4, 512), BF16), ((16, 4, 512), BF16),
        ((4, 16, 256), BF16), ((4, 16, 256), BF16), ((12, 4, 256), BF16), ((12, 4, 256), BF16),
        ((512, ROWS), BF16), ((512, ROWS), BF16), ((ROWS, WIDTH), BF16), ((n_depth, CAP, WIDTH), BF16),
        ((2, MIG, WIDTH), BF16), ((6, 2, 48, 128), F32),
        ((16, 4, 56, 128), F32), ((16, 4, 56, 128), F32), ((16, 4, 56, 128), F32),
        ((16, 4, 56, 128), F32), ((8, 4, 32, 128), F32),
        ((12, 2, 40, 128), F32), ((12, 2, 40, 128), F32), ((12, 2, 40, 128), F32), (row, F32),
    ]
    placed, species_next, order = pl.pallas_call(
        functools.partial(kernel, n_slab, n_depth),
        out_shape=(
            jax.ShapeDtypeStruct((8, 32, 512), F32),
            jax.ShapeDtypeStruct((n_depth * CAP + 2 * MIG, WIDTH), BF16),
            jax.ShapeDtypeStruct((512, 512), BF16),
        ),
        in_specs=[pl.BlockSpec(memory_space=pltpu.HBM)] * 10,
        out_specs=(vmem, vmem, vmem),
        scratch_shapes=[pltpu.VMEM(shape, dtype) for shape, dtype in scratch] + [
            pltpu.SemaphoreType.DMA((3, 8)), pltpu.SemaphoreType.DMA((3, 8)),
            pltpu.SemaphoreType.DMA((n_depth,)), pltpu.SemaphoreType.DMA((n_depth,)),
            pltpu.SemaphoreType.DMA((2,)), pltpu.SemaphoreType.DMA((2,)),
            pltpu.SemaphoreType.DMA((10,)),
        ],
        compiler_params=pltpu.CompilerParams(
            collective_id=0, has_side_effects=True, vmem_limit_bytes=48 * 1024 * 1024
        ),
        name="step",
    )(
        *[pltpu.with_memory_space_constraint(v, pltpu.HBM) for v in (nutrient, species, agent_cell.reshape(row), death_flag.reshape(row),
        divide_flag.reshape(row), slab_move.reshape(row), depth_route.reshape(row),
        net_weight, sensing.reshape(1, WIDTH), uptake_weight.reshape(1, WIDTH))],
    )
    return pl.pallas_call(
        finish,
        out_shape=(
            jax.ShapeDtypeStruct((8, 32, 512), F32),
            jax.ShapeDtypeStruct((n_depth * CAP + 2 * MIG, WIDTH), BF16),
        ),
        in_specs=[vmem] * 3,
        out_specs=(pl.BlockSpec(memory_space=pl.ANY), pl.BlockSpec(memory_space=pl.ANY)),
        scratch_shapes=[pltpu.VMEM((8, 32, 512), F32), pltpu.SemaphoreType.DMA((3,))],
        compiler_params=pltpu.CompilerParams(vmem_limit_bytes=16 * 1024 * 1024),
        name="finish",
    )(placed, species_next, order)


def solution(mesh):
    in_specs = (
        P("slab", "depth", None),
        P(("slab", "depth"), None),
        P(("slab", "depth")),
        P(("slab", "depth")),
        P(("slab", "depth")),
        P(("slab", "depth")),
        P(("slab", "depth"), None),
        P(),
        P(),
        P(),
    )
    out_specs = (P("slab", "depth", None), P(("slab", "depth"), None))
    body = functools.partial(local, mesh.shape["slab"], mesh.shape["depth"])
    return jax.shard_map(body, mesh=mesh, in_specs=in_specs, out_specs=out_specs, check_vma=False)
```

```python
import functools

import jax
import jax.numpy as jnp
from jax import lax
from jax.experimental import pallas as pl
from jax.experimental.pallas import tpu as pltpu
from jax.sharding import PartitionSpec as P

SCREENING = 0.05
DAMPING = 2.0 / 3.0
CENTRE = 6.0 + SCREENING
COARSE_CENTRE = 6.0 + 4.0 * SCREENING
F32 = jnp.float32
BF16 = jnp.bfloat16
I32 = jnp.int32
MESH = pl.DeviceIdType.MESH

ROWS = 1024
CAP = 256
MIG = 128
WIDTH = 128
SIDES = ((1, 0), (-1, 0), (0, 1), (0, -1), (1, 1), (1, -1), (-1, 1), (-1, -1))
ORDER = (4, 5, 6, 7, 0, 1, 2, 3)


def iota(shape, axis, dtype=I32):
    values = lax.broadcasted_iota(I32, shape, axis)
    return values if dtype == I32 else values.astype(dtype)


def tile_sweep(ref, x, tiles, first_row, rows, first_lane, last_lane):
    centre = [ref[x, z, pl.ds(first_row, rows), :] for z in range(tiles)]
    before_first = jnp.where(first_lane, 0.0, pltpu.roll(centre[-1], 1, 1))
    after_last = jnp.where(last_lane, 0.0, pltpu.roll(centre[0], 127, 1))
    out = []
    for z in range(tiles):
        total = centre[z - 1] if z > 0 else before_first
        total = total + (centre[z + 1] if z < tiles - 1 else after_last)
        total = total + ref[x, z, pl.ds(first_row - 1, rows), :]
        total = total + ref[x, z, pl.ds(first_row + 1, rows), :]
        total = total + ref[x - 1, z, pl.ds(first_row, rows), :]
        total = total + ref[x + 1, z, pl.ds(first_row, rows), :]
        out.append((centre[z], total))
    return out


def kernel(
    n_slab, n_depth,
    nut_in, spec_in, cell_in, death_in, divide_in, move_in, route_in, netw_in, sensing_in, uw_in,
    grid_out, spec_out, order,
    own_nb, nut, spec, cell, death, divide, move, route, netw, sensing, uw,
    nb, nb_low, nb_high, src, src_low, src_high, cb, cb_low, cb_high,
    xr_low, xr_high, yr_low, yr_high,
    xs_low, xs_high, ys_low, ys_high,
    xc_low, xc_high, yc_low, yc_high,
    lane_hot, cell_hot, upd, packed, movers, sbuf, tbuf, ubuf, vbuf, wbuf, rbuf, cbuf, dbuf, ebuf,
    sampled_row, halo_send, halo_recv, a2a_send, a2a_recv, mig_send, mig_recv, in_sem,
):
    s = lax.axis_index("slab")
    d = lax.axis_index("depth")

    def at(step_s, step_d):
        return (lax.rem(s + step_s + n_slab, n_slab), lax.rem(d + step_d + n_depth, n_depth))

    barrier = pltpu.get_barrier_semaphore()
    partners = [at(a, b) for a, b in SIDES if a != 0] + [at(0, k) for k in range(1, n_depth)]
    for partner in partners:
        pl.semaphore_signal(barrier, inc=1, device_id=partner, device_id_type=MESH)

    loads = []
    for i, (source_ref, target_ref) in enumerate((
        (cell_in, cell), (nut_in, nut), (spec_in, spec), (uw_in, uw), (death_in, death),
        (divide_in, divide), (move_in, move), (route_in, route), (netw_in, netw),
        (sensing_in, sensing),
    )):
        load = pltpu.make_async_copy(source_ref, target_ref, in_sem.at[i])
        load.start()
        loads.append(load)

    def exchange(number, sources, targets):
        copies = {}
        for i in ORDER:
            a, b = SIDES[i]
            copy = pltpu.make_async_remote_copy(
                src_ref=sources[i],
                dst_ref=targets[i],
                send_sem=halo_send.at[number, i],
                recv_sem=halo_recv.at[number, i],
                device_id=at(a, b),
                device_id_type=MESH,
            )
            copy.start()
            copies[i] = copy
        return [copies[i] for i in range(len(SIDES))]

    loads[0].wait()
    cell_row = cell[...]
    z_row = lax.rem(cell_row, 512)
    xy_row = lax.div(cell_row, 512)
    place_row = lax.rem(z_row, 4) * 128 + lax.div(z_row, 4)
    places = iota((1, 512), 1)
    cell_of_place = lax.rem(places, 128) * 4 + lax.div(places, 128)

    def fill_lane(i, carry):
        start = pl.multiple_of(i * 64, 64)
        hit = iota((64, ROWS), 0) == z_row - start
        lane_hot[pl.ds(start, 64), :] = jnp.where(hit, 1.0, 0.0).astype(BF16)
        hit = iota((64, ROWS), 0) == place_row - start
        cell_hot[pl.ds(start, 64), :] = jnp.where(hit, 1.0, 0.0).astype(BF16)
        hit = iota((64, 512), 0) == cell_of_place - start
        order[pl.ds(start, 64), :] = jnp.where(hit, 1.0, 0.0).astype(BF16)
        return carry

    lax.fori_loop(0, 8, fill_lane, 0)

    loads[1].wait()
    own_nb[...] = nut[...].reshape(256, 512).astype(BF16)
    placed = jnp.dot(own_nb[...], order[...], preferred_element_type=F32).astype(BF16)
    for x in range(8):
        plane = placed[x * 32:(x + 1) * 32]
        nb[x] = plane
        nb_low[x] = plane[0:4]
        nb_high[x] = plane[28:32]
    for load in loads[2:]:
        load.wait()
    own = pl.multiple_of(d * CAP, CAP)

    def gather_and_scatter():
        sampled = jnp.dot(own_nb[...], lane_hot[...], preferred_element_type=F32)
        row_hit = iota((256, ROWS), 0) == xy_row
        sample = jnp.sum(jnp.where(row_hit, sampled, 0.0), axis=0, keepdims=True)
        sampled_row[...] = sample
        alive = 1.0 - death[...].astype(F32)
        score = lax.dot_general(
            jnp.broadcast_to(uw[...], (16, WIDTH)), spec[...], (((1,), (1,)), ((), ())),
            preferred_element_type=F32,
        )[0:1]
        softplus = jnp.maximum(score, 0.0) + jnp.log1p(jnp.exp(-jnp.abs(score)))
        uptake = alive * (1.0 + divide[...].astype(F32)) * softplus * sample / (0.5 + sample)

        row_hit = iota((256, ROWS), 0) == xy_row
        source = lax.dot_general(
            jnp.where(row_hit, uptake, 0.0).astype(BF16), cell_hot[...], (((1,), (1,)), ((), ())),
            preferred_element_type=F32,
        ).reshape(8, 32, 512)
        for x in range(8):
            plane = source[x]
            rounded = plane.astype(BF16)
            src[x] = rounded
            src_low[x] = rounded[0:4]
            src_high[x] = rounded[28:32]
            for z in range(4):
                tbuf[4 + x, z, 12:44, :] = plane[:, z * 128:(z + 1) * 128]

    def species_work():
        sensed = sampled_row[...].astype(BF16).astype(F32)
        activation = jnp.dot(spec[...], netw[...], preferred_element_type=F32)
        sensed_column = jnp.transpose(jnp.broadcast_to(sensed, (WIDTH, ROWS)))
        activation = activation + sensed_column * sensing[...]
        upd[...] = (0.5 * spec[...].astype(F32) + jnp.tanh(activation)).astype(BF16)

        lanes = iota((16, ROWS), 0)
        move_row = move[...]
        route_row = route[...]
        counted = (lanes == route_row) | (lanes == 7 + move_row) & (move_row > 0)
        counted = jnp.where(counted, 1.0, 0.0)
        chosen = jnp.where(move_row == 0, route_row, 7 + move_row)
        stacked = jnp.concatenate([counted[:, a * 128:(a + 1) * 128] for a in range(8)], axis=0)
        before = jnp.where(iota((128, 128), 0) < iota((128, 128), 1), 1.0, 0.0)
        inside = jnp.dot(stacked.astype(BF16), before.astype(BF16), preferred_element_type=F32)
        total = jnp.dot(stacked.astype(BF16), jnp.ones((128, 128), BF16), preferred_element_type=F32)
        offset = jnp.zeros((16, 128), F32)
        ranks = []
        for a in range(8):
            ranks.append(inside[a * 16:(a + 1) * 16] + offset)
            offset = offset + total[a * 16:(a + 1) * 16]
        rank = jnp.concatenate(ranks, axis=1)
        rank = jnp.sum(jnp.where(lanes == chosen, rank, 0.0), axis=0, keepdims=True)
        rank = jnp.where(death[...] == 0, rank, -1.0)
        chosen = chosen.astype(F32)

        def pack(destination, slots):
            key = jnp.where(chosen == destination, rank, -1.0)
            hot = jnp.where(iota((slots, ROWS), 0, F32) == key, 1.0, 0.0).astype(BF16)
            return jnp.dot(hot, upd[...], preferred_element_type=F32).astype(BF16)

        def pack_step(k, carry):
            packed[k] = pack(lax.rem(d + k, n_depth).astype(F32), CAP)
            return carry

        lax.fori_loop(1, n_depth, pack_step, 0)
        movers[0] = pack(8.0, MIG)
        movers[1] = pack(9.0, MIG)
        spec_out[pl.ds(own, CAP), :] = pack(d.astype(F32), CAP)

    early = s == 0
    later = s > 0
    pl.when(early)(gather_and_scatter)
    pl.when(early & (d > 0))(species_work)

    pl.semaphore_wait(barrier, len(partners))
    first = exchange(
        0,
        [nb.at[pl.ds(4, 4)], nb.at[pl.ds(0, 4)], nb_high, nb_low,
         nb_high.at[pl.ds(5, 3)], nb_low.at[pl.ds(5, 3)],
         nb_high.at[pl.ds(0, 3)], nb_low.at[pl.ds(0, 3)]],
        [xr_low, xr_high, yr_low.at[pl.ds(4, 8)], yr_high.at[pl.ds(4, 8)],
         yr_low.at[pl.ds(1, 3)], yr_high.at[pl.ds(1, 3)],
         yr_low.at[pl.ds(12, 3)], yr_high.at[pl.ds(12, 3)]],
    )

    pl.when(later)(gather_and_scatter)
    second = exchange(
        1,
        [src.at[pl.ds(5, 3)], src.at[pl.ds(0, 3)], src_high, src_low,
         src_high.at[pl.ds(6, 2)], src_low.at[pl.ds(6, 2)],
         src_high.at[pl.ds(0, 2)], src_low.at[pl.ds(0, 2)]],
        [xs_low.at[pl.ds(1, 3)], xs_high.at[pl.ds(0, 3)],
         ys_low.at[pl.ds(4, 8)], ys_high.at[pl.ds(4, 8)],
         ys_low.at[pl.ds(2, 2)], ys_high.at[pl.ds(2, 2)],
         ys_low.at[pl.ds(12, 2)], ys_high.at[pl.ds(12, 2)]],
    )
    pl.when(later | (d == 0))(species_work)

    def send_block(k):
        return pltpu.make_async_remote_copy(
            src_ref=packed.at[k],
            dst_ref=spec_out.at[pl.ds(own, CAP), :],
            send_sem=a2a_send.at[k],
            recv_sem=a2a_recv.at[k],
            device_id=at(0, k),
            device_id_type=MESH,
        )

    blocks = [send_block(k) for k in (4, 3, 5, 2, 6, 1, 7)]

    def start_rest():
        for copy in blocks[3:]:
            copy.start()

    for copy in blocks[:3]:
        copy.start()
    pl.when(s < 4)(start_rest)

    for half in range(2):
        value = nut[4 * half:4 * half + 4].reshape(128, 512)
        rest = value - value.astype(BF16).astype(F32)
        piece = rest.astype(BF16)
        pieces = jnp.concatenate([piece, (rest - piece.astype(F32)).astype(BF16)], axis=0)
        rest = jnp.dot(pieces, order[...], preferred_element_type=F32)
        rest = rest[0:128] + rest[128:256]
        for i in range(4):
            x = 4 * half + i
            value = nb[x].astype(F32) + rest[i * 32:(i + 1) * 32]
            for z in range(4):
                part = value[:, z * 128:(z + 1) * 128]
                ubuf[4 + x, z, 12:44, :] = part
                tbuf[4 + x, z, 12:44, :] = SCREENING * part - tbuf[4 + x, z, 12:44, :]

    lane = iota((1, 128), 1)
    first_lane = lane == 0
    last_lane = lane == 127
    row8 = iota((8, 1), 0)
    keep_low = (row8 >= 4) | (d > 0)
    keep_high = (row8 < 4) | (d < n_depth - 1)
    has_low = jnp.full((4, 1), d, I32) > 0
    has_high = jnp.full((4, 1), d, I32) < n_depth - 1

    def fill_rows(x, with_source):
        low = jnp.where(has_low, yr_low[x].astype(F32), 0.0)
        high = jnp.where(has_high, yr_high[x].astype(F32), 0.0)
        for z in range(4):
            at_z = slice(z * 128, (z + 1) * 128)
            ubuf[x, z, 8:12, :] = low[:, at_z]
            ubuf[x, z, 44:48, :] = high[:, at_z]
        if with_source:
            low = SCREENING * low - ys_low[x].astype(F32)
            high = SCREENING * high - ys_high[x].astype(F32)
            for z in range(4):
                at_z = slice(z * 128, (z + 1) * 128)
                tbuf[x, z, 8:12, :] = low[:, at_z]
                tbuf[x, z, 44:48, :] = high[:, at_z]

    def masked(value, rows):
        return jnp.concatenate(
            [jnp.where(keep_low, value[0:8], 0.0), value[8:rows - 8],
             jnp.where(keep_high, value[rows - 8:], 0.0)], axis=0,
        )

    def sweep(source_ref, target_ref, x):
        for z, (value, around) in enumerate(
            tile_sweep(source_ref, x, 4, 8, 40, first_lane, last_lane)
        ):
            result = value * (1.0 - DAMPING) + (DAMPING / CENTRE) * (tbuf[x, z, 8:48, :] + around)
            target_ref[x, z, 8:48, :] = masked(result, 40)

    def residual(x):
        for z, (value, around) in enumerate(
            tile_sweep(wbuf, x, 4, 12, 32, first_lane, last_lane)
        ):
            rbuf[x - 4, z] = tbuf[x, z, 12:44, :] + around - CENTRE * value

    def loop(begin, end, step):
        lax.fori_loop(begin, end, lambda x, carry: (step(x), carry)[1], 0)

    for copy in (first[2], first[3], second[2], second[3]):
        copy.wait_recv()
    loop(4, 12, lambda x: fill_rows(x, True))
    loop(5, 11, lambda x: sweep(ubuf, vbuf, x))
    loop(6, 10, lambda x: sweep(vbuf, wbuf, x))
    loop(7, 9, residual)

    def fill_plane(x, value, taken):
        value = value.astype(F32)
        for z in range(4):
            ubuf[x, z, 12:44, :] = value[:, z * 128:(z + 1) * 128]
        if taken is not None:
            value = SCREENING * value - taken.astype(F32)
            for z in range(4):
                tbuf[x, z, 12:44, :] = value[:, z * 128:(z + 1) * 128]
        fill_rows(x, taken is not None)

    def both(step, offset):
        def run(x):
            step(x)
            step(x + offset)
        return run

    def low_side():
        for i in (0, 4, 5):
            first[i].wait_recv()
            second[i].wait_recv()
        fill_plane(0, xr_low[0], None)
        for i in range(1, 4):
            fill_plane(i, xr_low[i], xs_low[i])
        loop(1, 3, both(lambda x: sweep(ubuf, vbuf, x), 2))
        loop(2, 4, both(lambda x: sweep(vbuf, wbuf, x), 2))
        loop(4, 7, residual)

    def high_side():
        for i in (1, 6, 7):
            first[i].wait_recv()
            second[i].wait_recv()
        fill_plane(15, xr_high[3], None)
        for i in range(0, 3):
            fill_plane(12 + i, xr_high[i], xs_high[i])
        loop(11, 13, both(lambda x: sweep(ubuf, vbuf, x), 2))
        loop(10, 12, both(lambda x: sweep(vbuf, wbuf, x), 2))
        loop(9, 12, residual)

    @pl.when(s == n_slab - 1)
    def _():
        low_side()
        high_side()

    @pl.when(s < n_slab - 1)
    def _():
        high_side()
        low_side()

    def pair_sum(p, z):
        total = None
        for x in (2 * p, 2 * p + 1):
            for r in (0, 1):
                part = rbuf[x, z, pl.ds(r, 16, stride=2), :]
                total = part if total is None else total + part
        return total

    for h in range(2):
        at_h = slice(h * 128, (h + 1) * 128)
        for p in range(4):
            plane = 0.5 * (pair_sum(p, 2 * h) + pair_sum(p, 2 * h + 1))
            rounded = plane.astype(BF16)
            cb[p, :, at_h] = rounded
            cb_low[p, :, at_h] = rounded[0:4]
            cb_high[p, :, at_h] = rounded[12:16]
            cbuf[4 + p, h, 12:28, :] = plane
    third = exchange(
        2,
        [cb, cb, cb_high, cb_low, cb_high, cb_low, cb_high, cb_low],
        [xc_low, xc_high, yc_low.at[pl.ds(4, 4)], yc_high.at[pl.ds(4, 4)],
         yc_low.at[pl.ds(0, 4)], yc_high.at[pl.ds(0, 4)],
         yc_low.at[pl.ds(8, 4)], yc_high.at[pl.ds(8, 4)]],
    )
    pl.when(s >= 4)(start_rest)
    moved = []
    for i, step in enumerate((1, -1)):
        copy = pltpu.make_async_remote_copy(
            src_ref=movers.at[i],
            dst_ref=spec_out.at[pl.ds(n_depth * CAP + i * MIG, MIG), :],
            send_sem=mig_send.at[i],
            recv_sem=mig_recv.at[i],
            device_id=at(step, 0),
            device_id_type=MESH,
        )
        copy.start()
        moved.append(copy)
    for copy in third:
        copy.wait_recv()

    for p in range(12):
        low = jnp.where(has_low, yc_low[p].astype(F32), 0.0)
        high = jnp.where(has_high, yc_high[p].astype(F32), 0.0)
        for h in range(2):
            at_h = slice(h * 128, (h + 1) * 128)
            if p < 4:
                cbuf[p, h, 12:28, :] = xc_low[p, :, at_h].astype(F32)
            if p >= 8:
                cbuf[p, h, 12:28, :] = xc_high[p - 8, :, at_h].astype(F32)
            cbuf[p, h, 8:12, :] = low[:, at_h]
            cbuf[p, h, 28:32, :] = high[:, at_h]
    for p in range(12):
        for h in range(2):
            dbuf[p, h, 8:32, :] = (DAMPING / COARSE_CENTRE) * cbuf[p, h, 8:32, :]

    def coarse_sweep(source_ref, target_ref, p):
        for h, (value, around) in enumerate(
            tile_sweep(source_ref, p, 2, 8, 24, first_lane, last_lane)
        ):
            result = value * (1.0 - DAMPING) + (DAMPING / COARSE_CENTRE) * (
                cbuf[p, h, 8:32, :] + around
            )
            target_ref[p, h, 8:32, :] = masked(result, 24)

    loop(1, 6, both(lambda p: coarse_sweep(dbuf, ebuf, p), 5))
    loop(2, 6, both(lambda p: coarse_sweep(ebuf, dbuf, p), 4))
    loop(3, 6, both(lambda p: coarse_sweep(dbuf, ebuf, p), 3))

    for p in range(6):
        for h in range(2):
            part = ebuf[3 + p, h, 10:34, :]
            sbuf[p, h, pl.ds(0, 24, stride=2), :] = part
            sbuf[p, h, pl.ds(1, 24, stride=2), :] = part

    def correct(p):
        for h in range(2):
            addition = sbuf[p, h, 0:40, :]
            for x in (2 + 2 * p, 3 + 2 * p):
                for z in (2 * h, 2 * h + 1):
                    ubuf[x, z, 8:48, :] = wbuf[x, z, 8:48, :] + addition

    loop(0, 6, correct)
    loop(3, 8, both(lambda x: sweep(ubuf, vbuf, x), 5))

    def last_sweep(x):
        for z, (value, around) in enumerate(
            tile_sweep(vbuf, x, 4, 12, 32, first_lane, last_lane)
        ):
            grid_out[x - 4, :, z * 128:(z + 1) * 128] = value * (1.0 - DAMPING) + (
                DAMPING / CENTRE
            ) * (tbuf[x, z, 12:44, :] + around)

    loop(4, 8, both(last_sweep, 4))

    for copy in blocks + moved:
        copy.wait_recv()
    for copy in first + second + third + blocks + moved:
        copy.wait_send()


def finish(placed, species_next, order, grid_out, spec_out, grid, sem):
    copies = [pltpu.make_async_copy(species_next, spec_out, sem.at[0])]
    copies[0].start()
    for half in range(2):
        value = placed[4 * half:4 * half + 4].reshape(128, 512)
        piece = value.astype(BF16)
        rest = (value - piece.astype(F32)).astype(BF16)
        both = lax.dot_general(
            jnp.concatenate([piece, rest], axis=0), order[...], (((1,), (1,)), ((), ())),
            preferred_element_type=F32,
        )
        grid[4 * half:4 * half + 4] = (both[0:128] + both[128:256]).reshape(4, 32, 512)
        at_half = pl.ds(4 * half, 4)
        copies.append(pltpu.make_async_copy(grid.at[at_half], grid_out.at[at_half], sem.at[1 + half]))
        copies[-1].start()
    for copy in copies:
        copy.wait()


def local(n_slab, n_depth, nutrient, species, agent_cell, death_flag, divide_flag, slab_move,
          depth_route, net_weight, sensing, uptake_weight):
    row = (1, ROWS)
    vmem = pl.BlockSpec(memory_space=pltpu.VMEM)
    scratch = [
        ((256, 512), BF16),
        ((8, 32, 512), F32), ((ROWS, WIDTH), BF16), (row, I32), (row, I32), (row, I32), (row, I32),
        (row, I32), ((WIDTH, WIDTH), BF16), ((1, WIDTH), F32), ((1, WIDTH), BF16),
        ((8, 32, 512), BF16), ((8, 4, 512), BF16), ((8, 4, 512), BF16),
        ((8, 32, 512), BF16), ((8, 4, 512), BF16), ((8, 4, 512), BF16),
        ((4, 16, 256), BF16), ((4, 4, 256), BF16), ((4, 4, 256), BF16),
        ((4, 32, 512), BF16), ((4, 32, 512), BF16), ((16, 4, 512), BF16), ((16, 4, 512), BF16),
        ((4, 32, 512), BF16), ((4, 32, 512), BF16), ((16, 4, 512), BF16), ((16, 4, 512), BF16),
        ((4, 16, 256), BF16), ((4, 16, 256), BF16), ((12, 4, 256), BF16), ((12, 4, 256), BF16),
        ((512, ROWS), BF16), ((512, ROWS), BF16), ((ROWS, WIDTH), BF16), ((n_depth, CAP, WIDTH), BF16),
        ((2, MIG, WIDTH), BF16), ((6, 2, 48, 128), F32),
        ((16, 4, 56, 128), F32), ((16, 4, 56, 128), F32), ((16, 4, 56, 128), F32),
        ((16, 4, 56, 128), F32), ((8, 4, 32, 128), F32),
        ((12, 2, 40, 128), F32), ((12, 2, 40, 128), F32), ((12, 2, 40, 128), F32), (row, F32),
    ]
    placed, species_next, order = pl.pallas_call(
        functools.partial(kernel, n_slab, n_depth),
        out_shape=(
            jax.ShapeDtypeStruct((8, 32, 512), F32),
            jax.ShapeDtypeStruct((n_depth * CAP + 2 * MIG, WIDTH), BF16),
            jax.ShapeDtypeStruct((512, 512), BF16),
        ),
        in_specs=[pl.BlockSpec(memory_space=pltpu.HBM)] * 10,
        out_specs=(vmem, vmem, vmem),
        scratch_shapes=[pltpu.VMEM(shape, dtype) for shape, dtype in scratch] + [
            pltpu.SemaphoreType.DMA((3, 8)), pltpu.SemaphoreType.DMA((3, 8)),
            pltpu.SemaphoreType.DMA((n_depth,)), pltpu.SemaphoreType.DMA((n_depth,)),
            pltpu.SemaphoreType.DMA((2,)), pltpu.SemaphoreType.DMA((2,)),
            pltpu.SemaphoreType.DMA((10,)),
        ],
        compiler_params=pltpu.CompilerParams(
            collective_id=0, has_side_effects=True, vmem_limit_bytes=48 * 1024 * 1024
        ),
        name="step",
    )(
        *[pltpu.with_memory_space_constraint(v, pltpu.HBM) for v in (nutrient, species, agent_cell.reshape(row), death_flag.reshape(row),
        divide_flag.reshape(row), slab_move.reshape(row), depth_route.reshape(row),
        net_weight, sensing.reshape(1, WIDTH), uptake_weight.reshape(1, WIDTH))],
    )
    return pl.pallas_call(
        finish,
        out_shape=(
            jax.ShapeDtypeStruct((8, 32, 512), F32),
            jax.ShapeDtypeStruct((n_depth * CAP + 2 * MIG, WIDTH), BF16),
        ),
        in_specs=[vmem] * 3,
        out_specs=(pl.BlockSpec(memory_space=pl.ANY), pl.BlockSpec(memory_space=pl.ANY)),
        scratch_shapes=[pltpu.VMEM((8, 32, 512), F32), pltpu.SemaphoreType.DMA((3,))],
        compiler_params=pltpu.CompilerParams(vmem_limit_bytes=16 * 1024 * 1024),
        name="finish",
    )(placed, species_next, order)


def solution(mesh):
    in_specs = (
        P("slab", "depth", None),
        P(("slab", "depth"), None),
        P(("slab", "depth")),
        P(("slab", "depth")),
        P(("slab", "depth")),
        P(("slab", "depth")),
        P(("slab", "depth"), None),
        P(),
        P(),
        P(),
    )
    out_specs = (P("slab", "depth", None), P(("slab", "depth"), None))
    body = functools.partial(local, mesh.shape["slab"], mesh.shape["depth"])
    return jax.shard_map(body, mesh=mesh, in_specs=in_specs, out_specs=out_specs, check_vma=False)
```
